128 devices in a mesh: row: 16 (over y, x_lo, core), col: 8 (over z, x_hi).
Axes of the slice: x: 4 (x_hi: 2, x_lo: 2; x = x_hi * 2 + x_lo), y: 4, z: 4, core: 2. Of those that a mesh axis runs over, the one named last changes fastest.
Arguments:
- features: float32 [65536, 256], P(('col', 'row')), may hold values from -6 to 6
- weight_matrix: float32 [256, 256], replicated, may hold values from -0.375 to 0.375
- cotangent: float32 [65536, 256], P(('row', 'col')), may hold values from -6 to 6
- block_rows: int32 [16, 8, 96], P('row', 'col'), may hold values from 0 to 31
- block_cols: int32 [16, 8, 96], P('row', 'col'), may hold values from 0 to 63
- blocks: float32 [16, 8, 96, 128, 128], P('row', 'col'), may hold values from -0.109375 to 0.109375
Outputs:
- hidden: float32 [65536, 256], P(('row', 'col'))
- weight_grad: float32 [256, 256], replicated
- feature_grad: float32 [65536, 256], P(('col', 'row'))
The draws below stay inside these ranges and needn't reach their ends.
All inputs are finite; a program needn't handle non-finite values.
Results may differ from the reference program's by a relative error of at most 0.0001.
Values sent between devices are 32-bit elements; how exact they have to be, the bound alone decides.
A program may use at most 128 MiB of HBM per device.

```python
import math
import jax
import jax.numpy as jnp
import numpy as np
from jax import lax

F = 256
BS = 128
NB = 96
NODES = 65536
RB = 32
CB = 64
N_ROW = 16
N_COL = 8


def set_ends(array, key, smallest, top_value):
    spot = [jax.random.randint(jax.random.fold_in(key, axis), (), 0, length) for axis, length in enumerate(array.shape)]
    longest = array.shape.index(max(array.shape))
    next_to = spot[:longest] + [(spot[longest] + 1) % array.shape[longest]] + spot[longest + 1:]
    return array.at[tuple(spot)].set(smallest).at[tuple(next_to)].set(top_value)


def steps_of(rng, dims, split, smallest, high):
    loudness = 1.0
    for dim, parts in split:
        draws = jax.random.uniform(jax.random.fold_in(jax.random.fold_in(rng, 6), dim), (parts,), jnp.float32, smallest / len(split), high / len(split))
        loudness = loudness * jnp.repeat(jnp.exp(draws), dims[dim] // parts).reshape((-1,) + (1,) * (len(dims) - 1 - dim))
    return loudness


def rank_table(count, slope):
    weights = [(1 << 20) // math.isqrt(rank ** slope) + 1 for rank in range(1, count + 1)]
    scale = 1 + sum(weights) // (1 << 30)
    return np.cumsum(np.array([max(1, weight // scale) for weight in weights]))


def ranked_ids(key, extent, number_of, skew):
    grid = rank_table(number_of, skew)
    ticket = jax.random.randint(jax.random.fold_in(key, 1), extent, 0, int(grid[number_of - 1]))
    standing = jnp.searchsorted(jnp.asarray(grid, jnp.int32), ticket, side="right")
    return jax.random.permutation(jax.random.fold_in(key, 2), number_of)[standing].astype(jnp.int32)


def bell_draw(key, dims, scale, most, pieces=(), held_as=jnp.bfloat16):
    array = jax.random.normal(key, dims, jnp.float32) * scale
    if len(pieces) > 0:
        array = steps_of(key, dims, pieces, -0.22, 0.18) * array
    return jnp.clip(array, min=-most, max=most).astype(held_as)


def setup_inputs(seed: int = 0) -> dict:
    streams_of = jax.random.split(jax.random.key(seed), 7)
    features = bell_draw(streams_of[0], (NODES, F), 1.0, 6.0, ((0, 128),), jnp.float32)
    weight_matrix = bell_draw(streams_of[1], (F, F), F ** -0.5, 0.375, (), jnp.float32)
    cotangent = bell_draw(streams_of[2], (NODES, F), 1.0, 6.0, ((0, 128),), jnp.float32)
    block_rows = set_ends(ranked_ids(streams_of[3], (N_ROW, N_COL, NB), RB, 2), jax.random.fold_in(streams_of[3], 3), 0, RB - 1).astype(jnp.int32)
    block_cols = set_ends(jax.random.randint(streams_of[4], (N_ROW, N_COL, NB), 0, CB), jax.random.fold_in(streams_of[4], 1), 0, CB - 1).astype(jnp.int32)
    blocks = bell_draw(streams_of[5], (N_ROW, N_COL, NB, BS, BS), (BS * NB * N_COL // RB) ** -0.5, 0.109375, ((0, 16), (1, 8)), jnp.float32)
    return dict(features=features, weight_matrix=weight_matrix, cotangent=cotangent, block_rows=block_rows, block_cols=block_cols, blocks=blocks)


def activate(pre, cotangent):
    sigmoid_v = 1.0 / (1.0 + jnp.exp(-pre))
    return (pre * sigmoid_v, cotangent * sigmoid_v * (1.0 + pre * (1.0 - sigmoid_v)))

def reference(features, weight_matrix, cotangent, block_rows, block_cols, blocks):
    high = lax.Precision.HIGHEST
    total_blocks = NODES // BS
    row_base = (jnp.arange(N_ROW, dtype=jnp.int32) * RB)[:, None, None]
    col_base = (jnp.arange(N_COL, dtype=jnp.int32) * CB)[None, :, None]
    global_rows = (block_rows + row_base).reshape(N_ROW * N_COL, NB).astype(jnp.int32)
    global_cols = (block_cols + col_base).reshape(N_ROW * N_COL, NB).astype(jnp.int32)
    tile_values = blocks.reshape(N_ROW * N_COL, NB, BS, BS)

    def spread(source, take, put, form):
        source_blocks = source.reshape(total_blocks, BS, F)

        def step(total, item):
            take_ids, put_ids, values = item
            products = jnp.einsum(form, values, source_blocks[take_ids], precision=high)
            return (total.at[put_ids].add(products), None)
        start = jnp.zeros((total_blocks, BS, F), jnp.float32)
        total, unused = lax.scan(step, start, (take, put, tile_values))
        return total.reshape(NODES, F)
    aggregated = spread(features, global_cols, global_rows, 'kij,kjf->kif')
    pre = jnp.dot(aggregated, weight_matrix, precision=high)
    hidden, dpre = activate(pre, cotangent)
    weight_grad = jnp.dot(aggregated.T, dpre, precision=high) / jnp.sqrt(jnp.float32(NODES))
    back = jnp.dot(dpre, weight_matrix.T, precision=high)
    feature_grad = spread(back, global_rows, global_cols, 'kji,kjf->kif')
    return (hidden, weight_grad, feature_grad)
```

```python
import math
import jax
import jax.numpy as jnp
from jax import lax
from jax.experimental import pallas as pl
from jax.experimental.pallas import tpu as pltpu
from jax.sharding import PartitionSpec as P

F32 = jnp.float32
BF16 = jnp.bfloat16
MESH = pl.DeviceIdType.MESH
HA = 0
HB = 2
N_SEM = 192
FAR = 1 << 20


def split(value):
    high = value.astype(BF16)
    return high, (value - high.astype(F32)).astype(BF16)


def dot(a, b):
    return jnp.dot(a, b, preferred_element_type=F32)


def dot3(ah, al, bh, bl):
    return dot(ah, bh) + dot(al, bh) + dot(ah, bl)


def sort_tables(ids, table, base, scratch, other, sources):
    count = ids.shape[-1]
    scratch[...] = jnp.full(scratch.shape, FAR, jnp.int32)
    scratch[0:1, 0:count] = ids
    scratch[1:2, 0:count] = other
    lane_ids = jnp.broadcast_to(scratch[0:1, :], (128, 128))
    lane_other = jnp.broadcast_to(scratch[1:2, :], (128, 128))
    sub_ids, sub_other = lane_ids.T, lane_other.T
    lane = lax.broadcasted_iota(jnp.int32, (128, 128), 1)
    sub = lax.broadcasted_iota(jnp.int32, (128, 128), 0)

    def total(mask, value, axis):
        return jnp.sum(jnp.where(mask, value, 0), axis=axis, keepdims=True)

    rank = total((lane_ids < sub_ids) | ((lane_ids == sub_ids) & (lane < sub)), 1, 1)
    below = total(lane_ids < sub_ids, 1, 1)
    here = (jnp.broadcast_to(rank, (128, 128)) == lane) & (sub < count)
    order = total(here, sub, 0)
    source = total(here, sub_other, 0)
    starts = total(here, jnp.broadcast_to(below, (128, 128)), 0)
    upto = total(sub_ids <= lane, 1, 0)
    same = total(sub_ids == lane, 1, 0)
    table[base : base + 1, :] = jnp.clip(order, 0, count - 1)
    table[base + 1 : base + 2, :] = jnp.clip(source, 0, sources - 1)
    table[base + 2 : base + 3, :] = jnp.where(starts == lane[0:1, :], 1, 0)
    table[base + 3 : base + 4, :] = jnp.clip(upto - 1, 0, count - 1)
    table[base + 4 : base + 5, :] = jnp.where(same > 0, 1, 0)


class Links:
    def __init__(self, send_sem, recv_sem):
        self.send_sem, self.recv_sem, self.used, self.open = send_sem, recv_sem, 0, []

    def send(self, src, dst, device):
        i = self.used
        self.used += 1
        assert i < N_SEM
        copy = pltpu.make_async_remote_copy(
            src_ref=src, dst_ref=dst, send_sem=self.send_sem.at[i], recv_sem=self.recv_sem.at[i],
            device_id=device, device_id_type=MESH)
        copy.start()
        self.open.append(copy)
        return copy

    def flush(self):
        for copy in self.open:
            copy.wait_send()
        self.open = []


class GatherRing:
    def __init__(self, links, view, pos, plus, minus):
        self.links, self.view, self.pos, self.plus, self.minus = links, view, pos, plus, minus

    def start(self):
        view, q, send = self.view, self.pos, self.links.send
        a, b = view(q, HA, 2), view(q, HB, 2)
        self.c1 = send(a, a, self.plus)
        self.c2 = send(b, b, self.minus)
        self.c3 = send(b, b, self.plus)
        self.c4 = send(a, a, self.minus)

    def relay(self):
        view, q, send = self.view, self.pos, self.links.send
        left, right = lax.rem(q + 3, 4), lax.rem(q + 1, 4)
        self.c1.wait_recv()
        a = view(left, HA, 2)
        self.r1 = send(a, a, self.plus)
        self.c2.wait_recv()
        b = view(right, HB, 2)
        self.r2 = send(b, b, self.minus)

    def finish(self, arrived=None):
        view, q = self.view, self.pos
        self.c3.wait_recv()
        if arrived:
            arrived(view(lax.rem(q + 3, 4), HA, 4))
        self.c4.wait_recv()
        if arrived:
            arrived(view(lax.rem(q + 1, 4), HA, 4))
        self.r1.wait_recv()
        self.r2.wait_recv()
        if arrived:
            arrived(view(lax.rem(q + 2, 4), HA, 4))


class SumRing:
    def __init__(self, links, view, near, far, pos, plus, minus):
        self.links, self.view, self.near, self.far = links, view, near, far
        self.pos, self.plus, self.minus = pos, plus, minus

    def start(self):
        view, q, send = self.view, self.pos, self.links.send
        left, right, across = lax.rem(q + 3, 4), lax.rem(q + 1, 4), lax.rem(q + 2, 4)
        self.o1 = send(view(across, HA, 2), self.near.at[0], self.plus)
        self.o2 = send(view(across, HB, 2), self.near.at[1], self.minus)
        self.n1 = send(view(right, HB, 2), self.far.at[0, 2:4], self.plus)
        self.n2 = send(view(left, HA, 2), self.far.at[1, 0:2], self.minus)

    def relay(self):
        view, q, send = self.view, self.pos, self.links.send
        left, right = lax.rem(q + 3, 4), lax.rem(q + 1, 4)
        self.o1.wait_recv()
        part = view(right, HA, 2)
        part[...] += self.near[0]
        self.m1 = send(part, self.far.at[0, 0:2], self.plus)
        self.o2.wait_recv()
        part = view(left, HB, 2)
        part[...] += self.near[1]
        self.m2 = send(part, self.far.at[1, 2:4], self.minus)

    def finish(self):
        self.n1.wait_recv()
        self.n2.wait_recv()
        self.m1.wait_recv()
        self.m2.wait_recv()
        part = self.view(self.pos, HA, 4)
        part[...] += self.far[0] + self.far[1]
        return part


def kernel(total_nodes, feats, weight, cot, rows_in, cols_in, blocks, hidden_out, wgrad_out, fgrad_out,
           X, XX, A, AT, PS, OUT, BK, DR, CN, CF, CX, RN, RF, RX, W_ref, C_ref, AG, DP, HID, G, WH, WR, WS, WO,
           WP, IDS, TAB, TABS, send_sem, recv_sem, load_sem):
    row, col = lax.axis_index("row"), lax.axis_index("col")
    y, x_lo, core = row // 4, lax.rem(row // 2, 2), lax.rem(row, 2)
    z, x_hi = col // 2, lax.rem(col, 2)
    chip = row // 2

    def at_row(yy, xx, cc):
        return (yy * 4 + xx * 2 + cc, col)

    def at_col(zz, xx):
        return (row, zz * 2 + xx)

    y_plus, y_minus = at_row(lax.rem(y + 1, 4), x_lo, core), at_row(lax.rem(y + 3, 4), x_lo, core)
    z_plus, z_minus = at_col(lax.rem(z + 1, 4), x_hi), at_col(lax.rem(z + 3, 4), x_hi)
    x_near, twin, x_far = at_row(y, 1 - x_lo, core), at_row(y, x_lo, 1 - core), at_col(z, 1 - x_hi)
    col_peers = [(row, lax.rem(col + j, 8)) for j in range(1, 8)]
    row_peers = [(lax.rem(chip + j, 8) * 2 + core, col) for j in range(1, 8)]

    loads = []

    def load(src, dst):
        copy = pltpu.make_async_copy(src, dst, load_sem.at[len(loads)])
        copy.start()
        loads.append(copy)
        return copy

    lanes = [pl.ds(f * 128, 128) for f in range(2)]
    mine_x = [X.at[f, pl.ds(row * 4, 4)] for f in range(2)]
    get_x = [load(feats.at[:, :, lanes[f]], mine_x[f]) for f in range(2)]
    get_a = load(blocks, PS)
    get_w = load(weight, W_ref)
    get_c = load(cot, C_ref)

    barrier = pltpu.get_barrier_semaphore()
    peers = col_peers + row_peers + [twin]
    for peer in peers:
        pl.semaphore_signal(barrier, inc=1, device_id=peer, device_id_type=MESH)
    pl.semaphore_wait(barrier, len(peers))

    links = Links(send_sem, recv_sem)
    send = links.send

    def x_view(f, xx):
        return lambda q, half, n: X.at[f, pl.ds((q * 4 + xx * 2 + core) * 4 + half, n)]

    own = [GatherRing(links, x_view(f, x_lo), y, y_plus, y_minus) for f in range(2)]
    other = [GatherRing(links, x_view(f, 1 - x_lo), y, y_plus, y_minus) for f in range(2)]
    xs, twins = [None, None], [[], []]

    def to_twin(f):
        return lambda piece: twins[f].append(send(piece, piece, twin))

    get_x[0].wait()
    own[0].start()
    xs[0] = send(mine_x[0], mine_x[0], x_near)
    get_x[1].wait()
    xs[1] = send(mine_x[1], mine_x[1], x_near)
    to_twin(0)(mine_x[0])
    to_twin(1)(mine_x[1])

    sort_tables(rows_in[...], TAB, 0, IDS.at[0], cols_in[...], 64)
    sort_tables(cols_in[...], TAB, 8, IDS.at[1], rows_in[...], 32)
    get_tab = load(TAB, TABS)
    get_tab.wait()
    get_a.wait()

    def prepare(k, carry):
        value = PS[k]
        high, low = split(value)
        A[k, :, 0:128] = high
        A[k, :, 128:256] = low
        high, low = split(value.T)
        AT[k, :, 0:128] = high
        AT[k, :, 128:256] = low
        return carry

    lax.fori_loop(0, 32, prepare, 0)
    xs[0].wait_recv()
    other[0].start()
    to_twin(0)(x_view(0, 1 - x_lo)(y, HA, 4))
    lax.fori_loop(32, 64, prepare, 0)
    own[0].relay()
    other[0].relay()
    own[1].start()
    xs[1].wait_recv()
    other[1].start()
    to_twin(1)(x_view(1, 1 - x_lo)(y, HA, 4))
    lax.fori_loop(64, 96, prepare, 0)
    get_w.wait()
    high, low = split(W_ref[...])
    WP[0], WP[1] = high, low
    high, low = split(W_ref[...].T)
    WP[2], WP[3] = high, low
    get_c.wait()

    def to_pairs(source, f, count):
        def step(k, carry):
            high, low = split(source[f, k])
            XX[k, :, 0:128] = high
            XX[k, :, 128:256] = low
            return carry

        lax.fori_loop(0, count, step, 0, unroll=2)

    def tile_product(left, base):
        def step(p, total):
            lhs = left[TABS[base, p]]
            pair = XX[TABS[base + 1, p]]
            result = dot(lhs, jnp.concatenate([pair, pair], axis=0))
            term = result[:, 0:128] + result[:, 128:256]
            total = jnp.where(TABS[base + 2, p] == 1, term, total + term)
            PS[p] = total
            return total

        lax.fori_loop(0, PS.shape[0], step, jnp.zeros((128, 128), F32), unroll=4)

    def collect(dst, f, base, start, count, place):
        def step(r, carry):
            t = place(r)
            dst[f, t] = jnp.where(TABS[base + 4, t] == 1, PS[TABS[base + 3, t]], 0.0)
            return carry

        lax.fori_loop(start, start + count, step, 0, unroll=2)

    def same(r):
        return r

    def col_view(f, xx):
        return lambda q, half, n: OUT.at[f, pl.ds((q * 2 + xx) * 4 + half, n)]

    col_far = [SumRing(links, col_view(f, 1 - x_hi), CN.at[f, 0], CF.at[f, 0], z, z_plus, z_minus) for f in range(2)]
    col_own = [SumRing(links, col_view(f, x_hi), CN.at[f, 1], CF.at[f, 1], z, z_plus, z_minus) for f in range(2)]

    def finish_gather(f):
        own[f].finish(to_twin(f))
        other[f].finish(to_twin(f))
        for copy in twins[f]:
            copy.wait_recv()

    def forward(f):
        to_pairs(X, f, X.shape[1])
        tile_product(A, 0)
        collect(OUT, f, 0, 0, OUT.shape[1], same)
        col_far[f].start()
        col_own[f].start()

    finish_gather(0)
    forward(0)
    own[1].relay()
    other[1].relay()
    col_far[0].relay()
    col_own[0].relay()
    finish_gather(1)
    forward(1)
    sums = [None, None]
    sums[0] = send(col_far[0].finish(), CX.at[0], x_far)
    col_far[1].relay()
    col_own[1].relay()
    col_own[0].finish()
    sums[1] = send(col_far[1].finish(), CX.at[1], x_far)
    col_own[1].finish()
    for f in range(2):
        sums[f].wait_recv()

    def middle(i, carry):
        agg0 = OUT[0, col * 4 + i] + CX[0, i]
        agg1 = OUT[1, col * 4 + i] + CX[1, i]
        agg = jnp.concatenate([agg0, agg1], axis=1)
        ah, al = split(agg)
        pre = dot3(ah, al, WP[0], WP[1])
        sig = 1.0 / (1.0 + jnp.exp(-pre))
        HID[i] = pre * sig
        dpre = C_ref[i] * sig * (1.0 + pre * (1.0 - sig))
        dh, dl = split(dpre)
        back = dot3(dh, dl, WP[2], WP[3])
        BK[0, col * 4 + i] = back[:, 0:128]
        BK[1, col * 4 + i] = back[:, 128:256]
        AG[i] = agg
        DP[i] = dpre
        return carry

    lax.fori_loop(0, 4, middle, 0)

    def b_view(f, xx):
        return lambda q, half, n: BK.at[f, pl.ds((q * 2 + xx) * 4 + half, n)]

    own = [GatherRing(links, b_view(f, x_hi), z, z_plus, z_minus) for f in range(2)]
    other = [GatherRing(links, b_view(f, 1 - x_hi), z, z_plus, z_minus) for f in range(2)]
    mine_b = [BK.at[f, pl.ds(col * 4, 4)] for f in range(2)]
    own[0].start()
    xs = [send(mine_b[f], mine_b[f], x_far) for f in range(2)]
    put_h = load(HID, hidden_out)

    def term(i, total):
        th, tl = split(AG[i].T)
        dh, dl = split(DP[i])
        return total + dot3(th, tl, dh, dl)

    G[...] = lax.fori_loop(0, 4, term, jnp.zeros(G.shape, F32)) / jnp.float32(math.sqrt(total_nodes))
    half_of = lambda c: pl.ds(pl.multiple_of(c * 128, 128), 128)
    w1 = send(G.at[half_of(1 - core)], WH, twin)

    xs[0].wait_recv()
    other[0].start()
    w1.wait_recv()
    WH[...] += G[half_of(core), :]
    slot = lambda m: pl.ds(pl.multiple_of(m * 16, 16), 16)
    w2 = [send(WH.at[slot(peer[1])], WR.at[col], peer) for peer in col_peers]
    WR[col] = WH[slot(col), :]
    own[0].relay()
    other[0].relay()
    own[1].start()
    xs[1].wait_recv()
    other[1].start()
    for copy in w2:
        copy.wait_recv()

    def add_all(parts):
        total = parts[0]
        for m in range(1, 8):
            total = total + parts[m]
        return total

    WS[chip] = add_all(WR)
    w3 = [send(WS.at[chip], WS.at[chip], peer) for peer in row_peers]

    def r_view(f, xx):
        return lambda q, half, n: X.at[f, pl.ds((q * 4 + xx * 2 + core) * 4 + half, n)]

    row_far = [SumRing(links, r_view(f, 1 - x_lo), RN.at[f, 0], RF.at[f, 0], y, y_plus, y_minus) for f in range(2)]
    row_own = [SumRing(links, r_view(f, x_lo), RN.at[f, 1], RF.at[f, 1], y, y_plus, y_minus) for f in range(2)]

    def finish_back(f):
        own[f].finish()
        other[f].finish()

    links.flush()

    def backward(f):
        to_pairs(BK, f, BK.shape[1])
        tile_product(AT, 8)

        def part(c):
            return lambda r: (r // 4) * 8 + c * 4 + lax.rem(r, 4)

        collect(X, f, 8, 0, 32, part(1 - core))
        moves = []
        for m in range(8):
            b = m * 8 + (1 - core) * 4
            moves.append(send(X.at[f, pl.ds(b, 4)], DR.at[f, pl.ds(m * 4, 4)], twin))
        collect(X, f, 8, 0, 32, part(core))
        return moves

    def join(f, moves):
        for copy in moves:
            copy.wait_recv()

        def step(r, carry):
            t = (r // 4) * 8 + core * 4 + lax.rem(r, 4)
            X[f, t] += DR[f, r]
            return carry

        lax.fori_loop(0, 32, step, 0, unroll=2)
        row_far[f].start()
        row_own[f].start()

    finish_back(0)
    moves = backward(0)
    own[1].relay()
    other[1].relay()
    join(0, moves)
    for copy in w3:
        copy.wait_recv()
    mine_w = WO.at[pl.ds(pl.multiple_of(core * 128 + col * 16, 16), 16)]
    mine_w[...] = add_all(WS)
    w4 = [send(mine_w, mine_w, peer) for peer in col_peers]
    row_far[0].relay()
    row_own[0].relay()
    finish_back(1)
    moves = backward(1)
    for copy in w4:
        copy.wait_recv()
    w5 = send(WO.at[half_of(core)], WO.at[half_of(core)], twin)
    sums[0] = send(row_far[0].finish(), RX.at[0], x_near)
    join(1, moves)
    row_own[0].finish()
    row_far[1].relay()
    row_own[1].relay()
    w5.wait_recv()
    put_w = load(WO, wgrad_out)
    sums[1] = send(row_far[1].finish(), RX.at[1], x_near)
    sums[0].wait_recv()
    mine_x[0][...] += RX[0]
    put_0 = load(mine_x[0], fgrad_out.at[:, :, lanes[0]])
    row_own[1].finish()
    sums[1].wait_recv()
    mine_x[1][...] += RX[1]
    put_1 = load(mine_x[1], fgrad_out.at[:, :, lanes[1]])
    links.flush()
    for copy in (put_h, put_w, put_0, put_1):
        copy.wait()


def shards(features, weight_matrix, cotangent, block_rows, block_cols, blocks):
    assert lax.axis_size("row") == 16 and lax.axis_size("col") == 8
    count = blocks.shape[2]
    rows_dev, width = features.shape
    assert (rows_dev, width) == (512, 256) and blocks.shape[3] == 128 and count <= 128
    total_nodes = rows_dev * 128
    any_ = pl.BlockSpec(memory_space=pl.ANY)
    vmem = pl.BlockSpec(memory_space=pltpu.VMEM)
    out = [
        jax.ShapeDtypeStruct((4, 128, 256), F32),
        jax.ShapeDtypeStruct((256, 256), F32),
        jax.ShapeDtypeStruct((4, 128, 256), F32),
    ]
    scratch = [
        pltpu.VMEM((2, 64, 128, 128), F32),
        pltpu.VMEM((64, 128, 256), BF16),
        pltpu.VMEM((count, 128, 256), BF16),
        pltpu.VMEM((count, 128, 256), BF16),
        pltpu.VMEM((count, 128, 128), F32),
        pltpu.VMEM((2, 32, 128, 128), F32),
        pltpu.VMEM((2, 32, 128, 128), F32),
        pltpu.VMEM((2, 32, 128, 128), F32),
        pltpu.VMEM((2, 2, 2, 2, 128, 128), F32),
        pltpu.VMEM((2, 2, 2, 4, 128, 128), F32),
        pltpu.VMEM((2, 4, 128, 128), F32),
        pltpu.VMEM((2, 2, 2, 2, 128, 128), F32),
        pltpu.VMEM((2, 2, 2, 4, 128, 128), F32),
        pltpu.VMEM((2, 4, 128, 128), F32),
        pltpu.VMEM((256, 256), F32),
        pltpu.VMEM((4, 128, 256), F32),
        pltpu.VMEM((4, 128, 256), F32),
        pltpu.VMEM((4, 128, 256), F32),
        pltpu.VMEM((4, 128, 256), F32),
        pltpu.VMEM((256, 256), F32),
        pltpu.VMEM((128, 256), F32),
        pltpu.VMEM((8, 16, 256), F32),
        pltpu.VMEM((8, 16, 256), F32),
        pltpu.VMEM((256, 256), F32),
        pltpu.VMEM((4, 256, 256), BF16),
        pltpu.VMEM((2, 8, 128), jnp.int32),
        pltpu.VMEM((16, 128), jnp.int32),
        pltpu.SMEM((16, 128), jnp.int32),
        pltpu.SemaphoreType.DMA((N_SEM,)),
        pltpu.SemaphoreType.DMA((N_SEM,)),
        pltpu.SemaphoreType.DMA((16,)),
    ]
    hidden, weight_grad, feature_grad = pl.pallas_call(
        lambda *refs: kernel(total_nodes, *refs),
        out_shape=out,
        in_specs=[any_, any_, any_, vmem, vmem, any_],
        out_specs=[any_] * 3,
        scratch_shapes=scratch,
        compiler_params=pltpu.CompilerParams(
            collective_id=0, has_side_effects=True, vmem_limit_bytes=63 * 1024 * 1024
        ),
        name="graph_layer",
    )(
        features.reshape(4, 128, width),
        weight_matrix,
        cotangent.reshape(4, 128, width),
        block_rows[0],
        block_cols[0],
        blocks[0, 0],
    )
    return hidden.reshape(rows_dev, width), weight_grad, feature_grad.reshape(rows_dev, width)


def solution(mesh):
    in_specs = (
        P(("col", "row"), None),
        P(),
        P(("row", "col"), None),
        P("row", "col", None),
        P("row", "col", None),
        P("row", "col", None, None, None),
    )
    out_specs = (P(("row", "col"), None), P(), P(("col", "row"), None))
    return jax.shard_map(shards, mesh=mesh, in_specs=in_specs, out_specs=out_specs, check_vma=False)
```

```python
import math
import jax
import jax.numpy as jnp
from jax import lax
from jax.experimental import pallas as pl
from jax.experimental.pallas import tpu as pltpu
from jax.sharding import PartitionSpec as P

F32 = jnp.float32
BF16 = jnp.bfloat16
MESH = pl.DeviceIdType.MESH
HA = 0
HB = 2
N_SEM = 192
FAR = 1 << 20


def split(value):
    high = value.astype(BF16)
    return high, (value - high.astype(F32)).astype(BF16)


def dot(a, b):
    return jnp.dot(a, b, preferred_element_type=F32)


def dot3(ah, al, bh, bl):
    return dot(ah, bh) + dot(al, bh) + dot(ah, bl)


def sort_tables(ids, table, base, scratch, other, sources):
    count = ids.shape[-1]
    scratch[...] = jnp.full(scratch.shape, FAR, jnp.int32)
    scratch[0:1, 0:count] = ids
    scratch[1:2, 0:count] = other
    lane_ids = jnp.broadcast_to(scratch[0:1, :], (128, 128))
    lane_other = jnp.broadcast_to(scratch[1:2, :], (128, 128))
    sub_ids, sub_other = lane_ids.T, lane_other.T
    lane = lax.broadcasted_iota(jnp.int32, (128, 128), 1)
    sub = lax.broadcasted_iota(jnp.int32, (128, 128), 0)

    def total(mask, value, axis):
        return jnp.sum(jnp.where(mask, value, 0), axis=axis, keepdims=True)

    rank = total((lane_ids < sub_ids) | ((lane_ids == sub_ids) & (lane < sub)), 1, 1)
    below = total(lane_ids < sub_ids, 1, 1)
    here = (jnp.broadcast_to(rank, (128, 128)) == lane) & (sub < count)
    order = total(here, sub, 0)
    source = total(here, sub_other, 0)
    starts = total(here, jnp.broadcast_to(below, (128, 128)), 0)
    upto = total(sub_ids <= lane, 1, 0)
    same = total(sub_ids == lane, 1, 0)
    table[base : base + 1, :] = jnp.clip(order, 0, count - 1)
    table[base + 1 : base + 2, :] = jnp.clip(source, 0, sources - 1)
    table[base + 2 : base + 3, :] = jnp.where(starts == lane[0:1, :], 1, 0)
    table[base + 3 : base + 4, :] = jnp.clip(upto - 1, 0, count - 1)
    table[base + 4 : base + 5, :] = jnp.where(same > 0, 1, 0)


class Links:
    def __init__(self, send_sem, recv_sem):
        self.send_sem, self.recv_sem, self.used, self.open = send_sem, recv_sem, 0, []

    def send(self, src, dst, device):
        i = self.used
        self.used += 1
        assert i < N_SEM
        copy = pltpu.make_async_remote_copy(
            src_ref=src, dst_ref=dst, send_sem=self.send_sem.at[i], recv_sem=self.recv_sem.at[i],
            device_id=device, device_id_type=MESH)
        copy.start()
        self.open.append(copy)
        return copy

    def flush(self):
        for copy in self.open:
            copy.wait_send()
        self.open = []


class GatherRing:
    def __init__(self, links, view, pos, plus, minus):
        self.links, self.view, self.pos, self.plus, self.minus = links, view, pos, plus, minus

    def start(self, halves=(None, None)):
        view, q, send = self.view, self.pos, self.links.send
        a, b = view(q, HA, 2), view(q, HB, 2)
        if halves[0]:
            halves[0].wait_recv()
        self.c1 = send(a, a, self.plus)
        if halves[0]:
            self.c4 = send(a, a, self.minus)
            halves[1].wait_recv()
        self.c2 = send(b, b, self.minus)
        self.c3 = send(b, b, self.plus)
        if not halves[0]:
            self.c4 = send(a, a, self.minus)

    def relay(self):
        view, q, send = self.view, self.pos, self.links.send
        left, right = lax.rem(q + 3, 4), lax.rem(q + 1, 4)
        self.c1.wait_recv()
        a = view(left, HA, 2)
        self.r1 = send(a, a, self.plus)
        self.c2.wait_recv()
        b = view(right, HB, 2)
        self.r2 = send(b, b, self.minus)

    def finish(self, arrived=None):
        view, q = self.view, self.pos
        self.c3.wait_recv()
        if arrived:
            arrived(view(lax.rem(q + 3, 4), HA, 4))
        self.c4.wait_recv()
        if arrived:
            arrived(view(lax.rem(q + 1, 4), HA, 4))
        self.r1.wait_recv()
        self.r2.wait_recv()
        if arrived:
            arrived(view(lax.rem(q + 2, 4), HA, 4))


class SumRing:
    def __init__(self, links, view, near, far, pos, plus, minus):
        self.links, self.view, self.near, self.far = links, view, near, far
        self.pos, self.plus, self.minus = pos, plus, minus

    def start(self):
        view, q, send = self.view, self.pos, self.links.send
        left, right, across = lax.rem(q + 3, 4), lax.rem(q + 1, 4), lax.rem(q + 2, 4)
        self.o1 = send(view(across, HA, 2), self.near.at[0], self.plus)
        self.o2 = send(view(across, HB, 2), self.near.at[1], self.minus)
        self.n1 = send(view(right, HB, 2), self.far.at[0, 2:4], self.plus)
        self.n2 = send(view(left, HA, 2), self.far.at[1, 0:2], self.minus)

    def relay(self):
        view, q, send = self.view, self.pos, self.links.send
        left, right = lax.rem(q + 3, 4), lax.rem(q + 1, 4)
        self.o1.wait_recv()
        part = view(right, HA, 2)
        part[...] += self.near[0]
        self.m1 = send(part, self.far.at[0, 0:2], self.plus)
        self.o2.wait_recv()
        part = view(left, HB, 2)
        part[...] += self.near[1]
        self.m2 = send(part, self.far.at[1, 2:4], self.minus)

    def finish(self):
        self.n1.wait_recv()
        self.n2.wait_recv()
        self.m1.wait_recv()
        self.m2.wait_recv()
        part = self.view(self.pos, HA, 4)
        part[...] += self.far[0] + self.far[1]
        return part


def kernel(total_nodes, feats, weight, cot, rows_in, cols_in, blocks, hidden_out, wgrad_out, fgrad_out,
           X, XX, A, AT, PS, OUT, BK, DR, CN, CF, CX, RN, RF, RX, W_ref, C_ref, AG, DP, HID, G, WH, WR, WS, WO,
           WP, IDS, TAB, TABS, send_sem, recv_sem, load_sem):
    row, col = lax.axis_index("row"), lax.axis_index("col")
    y, x_lo, core = row // 4, lax.rem(row // 2, 2), lax.rem(row, 2)
    z, x_hi = col // 2, lax.rem(col, 2)
    chip = row // 2

    def at_row(yy, xx, cc):
        return (yy * 4 + xx * 2 + cc, col)

    def at_col(zz, xx):
        return (row, zz * 2 + xx)

    y_plus, y_minus = at_row(lax.rem(y + 1, 4), x_lo, core), at_row(lax.rem(y + 3, 4), x_lo, core)
    z_plus, z_minus = at_col(lax.rem(z + 1, 4), x_hi), at_col(lax.rem(z + 3, 4), x_hi)
    x_near, twin, x_far = at_row(y, 1 - x_lo, core), at_row(y, x_lo, 1 - core), at_col(z, 1 - x_hi)
    col_peers = [(row, lax.rem(col + j, 8)) for j in range(1, 8)]
    row_peers = [(lax.rem(chip + j, 8) * 2 + core, col) for j in range(1, 8)]

    loads = []

    def load(src, dst):
        copy = pltpu.make_async_copy(src, dst, load_sem.at[len(loads)])
        copy.start()
        loads.append(copy)
        return copy

    lanes = [pl.ds(f * 128, 128) for f in range(2)]
    mine_x = [X.at[f, pl.ds(row * 4, 4)] for f in range(2)]
    get_x = [load(feats.at[:, :, lanes[f]], mine_x[f]) for f in range(2)]
    get_a = load(blocks, PS)
    get_w = load(weight, W_ref)
    get_c = load(cot, C_ref)

    barrier = pltpu.get_barrier_semaphore()
    peers = col_peers + row_peers + [twin]
    for peer in peers:
        pl.semaphore_signal(barrier, inc=1, device_id=peer, device_id_type=MESH)
    pl.semaphore_wait(barrier, len(peers))

    links = Links(send_sem, recv_sem)
    send = links.send

    def x_view(f, xx):
        return lambda q, half, n: X.at[f, pl.ds((q * 4 + xx * 2 + core) * 4 + half, n)]

    own = [GatherRing(links, x_view(f, x_lo), y, y_plus, y_minus) for f in range(2)]
    other = [GatherRing(links, x_view(f, 1 - x_lo), y, y_plus, y_minus) for f in range(2)]
    xs, twins = [None, None], [[], []]

    def to_twin(f):
        return lambda piece: twins[f].append(send(piece, piece, twin))

    def across(view, pos, device):
        return [send(view(pos, half, 2), view(pos, half, 2), device) for half in (HA, HB)]

    get_x[0].wait()
    xs[0] = across(x_view(0, x_lo), y, x_near)
    own[0].start()
    get_x[1].wait()
    xs[1] = across(x_view(1, x_lo), y, x_near)
    to_twin(0)(mine_x[0])
    to_twin(1)(mine_x[1])

    sort_tables(rows_in[...], TAB, 0, IDS.at[0], cols_in[...], 64)
    sort_tables(cols_in[...], TAB, 8, IDS.at[1], rows_in[...], 32)
    get_tab = load(TAB, TABS)
    get_tab.wait()
    get_a.wait()

    def prepare(k, carry):
        value = PS[k]
        high, low = split(value)
        A[k, :, 0:128] = high
        A[k, :, 128:256] = low
        high, low = split(value.T)
        AT[k, :, 0:128] = high
        AT[k, :, 128:256] = low
        return carry

    lax.fori_loop(0, 16, prepare, 0)
    other[0].start(xs[0])
    to_twin(0)(x_view(0, 1 - x_lo)(y, HA, 4))
    lax.fori_loop(16, 32, prepare, 0)
    own[0].relay()
    lax.fori_loop(32, 48, prepare, 0)
    other[0].relay()
    own[1].start()
    other[1].start(xs[1])
    to_twin(1)(x_view(1, 1 - x_lo)(y, HA, 4))
    lax.fori_loop(48, 96, prepare, 0)
    get_w.wait()
    high, low = split(W_ref[...])
    WP[0], WP[1] = high, low
    high, low = split(W_ref[...].T)
    WP[2], WP[3] = high, low
    get_c.wait()

    def to_pairs(source, f, count):
        def step(k, carry):
            high, low = split(source[f, k])
            XX[k, :, 0:128] = high
            XX[k, :, 128:256] = low
            return carry

        lax.fori_loop(0, count, step, 0, unroll=2)

    def tile_product(left, base):
        def step(p, total):
            lhs = left[TABS[base, p]]
            pair = XX[TABS[base + 1, p]]
            result = dot(lhs, jnp.concatenate([pair, pair], axis=0))
            term = result[:, 0:128] + result[:, 128:256]
            total = jnp.where(TABS[base + 2, p] == 1, term, total + term)
            PS[p] = total
            return total

        lax.fori_loop(0, PS.shape[0], step, jnp.zeros((128, 128), F32), unroll=4)

    def collect(dst, f, base, start, count, place):
        def step(r, carry):
            t = place(r)
            dst[f, t] = jnp.where(TABS[base + 4, t] == 1, PS[TABS[base + 3, t]], 0.0)
            return carry

        lax.fori_loop(start, start + count, step, 0, unroll=2)

    def same(r):
        return r

    def col_view(f, xx):
        return lambda q, half, n: OUT.at[f, pl.ds((q * 2 + xx) * 4 + half, n)]

    col_far = [SumRing(links, col_view(f, 1 - x_hi), CN.at[f, 0], CF.at[f, 0], z, z_plus, z_minus) for f in range(2)]
    col_own = [SumRing(links, col_view(f, x_hi), CN.at[f, 1], CF.at[f, 1], z, z_plus, z_minus) for f in range(2)]

    def finish_gather(f):
        own[f].finish(to_twin(f))
        other[f].finish(to_twin(f))
        for copy in twins[f]:
            copy.wait_recv()

    def forward(f):
        to_pairs(X, f, X.shape[1])
        tile_product(A, 0)
        collect(OUT, f, 0, 0, OUT.shape[1], same)
        col_far[f].start()

    finish_gather(0)
    forward(0)
    own[1].relay()
    col_far[0].relay()
    col_own[0].start()
    other[1].relay()
    finish_gather(1)
    sums = [send(col_far[0].finish(), CX.at[0], x_far)]
    col_own[0].relay()
    forward(1)
    col_own[0].finish()
    col_far[1].relay()
    col_own[1].start()
    sums.append(send(col_far[1].finish(), CX.at[1], x_far))
    col_own[1].relay()
    col_own[1].finish()
    for f in range(2):
        sums[f].wait_recv()

    early, links.open = links.open, []

    def middle(i, carry):
        agg0 = OUT[0, col * 4 + i] + CX[0, i]
        agg1 = OUT[1, col * 4 + i] + CX[1, i]
        agg = jnp.concatenate([agg0, agg1], axis=1)
        ah, al = split(agg)
        pre = dot3(ah, al, WP[0], WP[1])
        sig = 1.0 / (1.0 + jnp.exp(-pre))
        HID[i] = pre * sig
        dpre = C_ref[i] * sig * (1.0 + pre * (1.0 - sig))
        dh, dl = split(dpre)
        back = dot3(dh, dl, WP[2], WP[3])
        BK[0, col * 4 + i] = back[:, 0:128]
        BK[1, col * 4 + i] = back[:, 128:256]
        AG[i] = agg
        DP[i] = dpre
        return carry

    lax.fori_loop(0, 4, middle, 0)

    def b_view(f, xx):
        return lambda q, half, n: BK.at[f, pl.ds((q * 2 + xx) * 4 + half, n)]

    own = [GatherRing(links, b_view(f, x_hi), z, z_plus, z_minus) for f in range(2)]
    other = [GatherRing(links, b_view(f, 1 - x_hi), z, z_plus, z_minus) for f in range(2)]
    xs = [across(b_view(0, x_hi), z, x_far)]
    own[0].start()
    xs.append(across(b_view(1, x_hi), z, x_far))
    put_h = load(HID, hidden_out)

    def term(i, total):
        th, tl = split(AG[i].T)
        dh, dl = split(DP[i])
        return total + dot3(th, tl, dh, dl)

    G[...] = lax.fori_loop(0, 4, term, jnp.zeros(G.shape, F32)) / jnp.float32(math.sqrt(total_nodes))
    half_of = lambda c: pl.ds(pl.multiple_of(c * 128, 128), 128)
    w1 = send(G.at[half_of(1 - core)], WH, twin)

    other[0].start(xs[0])
    w1.wait_recv()
    WH[...] += G[half_of(core), :]
    slot = lambda m: pl.ds(pl.multiple_of(m * 16, 16), 16)
    w2 = [send(WH.at[slot(peer[1])], WR.at[col], peer) for peer in col_peers]
    WR[col] = WH[slot(col), :]
    own[0].relay()
    other[0].relay()
    own[1].start()
    other[1].start(xs[1])
    for copy in w2:
        copy.wait_recv()

    def add_all(parts):
        total = parts[0]
        for m in range(1, 8):
            total = total + parts[m]
        return total

    WS[chip] = add_all(WR)
    w3 = [send(WS.at[chip], WS.at[chip], peer) for peer in row_peers]

    def r_view(f, xx, cc):
        return lambda q, half, n: X.at[f, pl.ds((q * 4 + xx * 2 + cc) * 4 + half, n)]

    def part(xx, cc):
        return lambda r: ((r // 4) * 4 + xx * 2 + cc) * 4 + lax.rem(r, 4)

    row_far = [SumRing(links, r_view(f, 1 - x_lo, core), RN.at[f, 0], RF.at[f, 0], y, y_plus, y_minus) for f in range(2)]
    row_own = [SumRing(links, r_view(f, x_lo, core), RN.at[f, 1], RF.at[f, 1], y, y_plus, y_minus) for f in range(2)]

    def finish_back(f):
        own[f].finish()
        other[f].finish()

    for copy in early:
        copy.wait_send()

    def backward(f):
        to_pairs(BK, f, BK.shape[1])
        tile_product(AT, 8)

        moves = []
        for k, xx in enumerate((1 - x_lo, x_lo)):
            collect(X, f, 8, 0, 16, part(xx, 1 - core))
            for m in range(4):
                moves.append(send(r_view(f, xx, 1 - core)(m, HA, 4), DR.at[f, pl.ds(k * 16 + m * 4, 4)], twin))
        for xx in (1 - x_lo, x_lo):
            collect(X, f, 8, 0, 16, part(xx, core))
        return moves

    def join(f, moves, k):
        for copy in moves[k * 4 : k * 4 + 4]:
            copy.wait_recv()
        place = part(x_lo if k else 1 - x_lo, core)

        def step(r, carry):
            X[f, place(r)] += DR[f, k * 16 + r]
            return carry

        lax.fori_loop(0, 16, step, 0, unroll=2)

    finish_back(0)
    moves = backward(0)
    own[1].relay()
    join(0, moves, 0)
    row_far[0].start()
    join(0, moves, 1)
    other[1].relay()
    for copy in w3:
        copy.wait_recv()
    mine_w = WO.at[pl.ds(pl.multiple_of(core * 128 + col * 16, 16), 16)]
    mine_w[...] = add_all(WS)
    w4 = [send(mine_w, mine_w, peer) for peer in col_peers]
    row_far[0].relay()
    row_own[0].start()
    finish_back(1)
    moves = backward(1)
    row_own[0].relay()
    sums = [send(row_far[0].finish(), RX.at[0], x_near)]
    join(1, moves, 0)
    row_far[1].start()
    join(1, moves, 1)
    for copy in w4:
        copy.wait_recv()
    w5 = send(WO.at[half_of(core)], WO.at[half_of(core)], twin)
    row_own[0].finish()
    row_far[1].relay()
    row_own[1].start()
    w5.wait_recv()
    put_w = load(WO, wgrad_out)
    sums[0].wait_recv()
    mine_x[0][...] += RX[0]
    put_0 = load(mine_x[0], fgrad_out.at[:, :, lanes[0]])
    sums.append(send(row_far[1].finish(), RX.at[1], x_near))
    row_own[1].relay()
    row_own[1].finish()
    sums[1].wait_recv()
    mine_x[1][...] += RX[1]
    put_1 = load(mine_x[1], fgrad_out.at[:, :, lanes[1]])
    links.flush()
    for copy in (put_h, put_w, put_0, put_1):
        copy.wait()


def hand_over(*refs):
    count = len(refs) // 3
    sources, results, held = refs[:count], refs[count : 2 * count], refs[2 * count : 3 * count]
    in_sem, out_sem = refs[3 * count :]
    ins = [pltpu.make_async_copy(sources[i], held[i], in_sem.at[i]) for i in range(count)]
    outs = [pltpu.make_async_copy(held[i], results[i], out_sem.at[i]) for i in range(count)]
    for copy in ins:
        copy.start()
    for i in range(count):
        ins[i].wait()
        outs[i].start()
    for copy in outs:
        copy.wait()


def shards(features, weight_matrix, cotangent, block_rows, block_cols, blocks):
    assert lax.axis_size("row") == 16 and lax.axis_size("col") == 8
    count = blocks.shape[2]
    rows_dev, width = features.shape
    assert (rows_dev, width) == (512, 256) and blocks.shape[3] == 128 and count <= 128
    total_nodes = rows_dev * 128
    any_ = pl.BlockSpec(memory_space=pl.ANY)
    vmem = pl.BlockSpec(memory_space=pltpu.VMEM)
    out = [
        jax.ShapeDtypeStruct((4, 128, 256), F32),
        jax.ShapeDtypeStruct((256, 256), F32),
        jax.ShapeDtypeStruct((4, 128, 256), F32),
    ]
    scratch = [
        pltpu.VMEM((2, 64, 128, 128), F32),
        pltpu.VMEM((64, 128, 256), BF16),
        pltpu.VMEM((count, 128, 256), BF16),
        pltpu.VMEM((count, 128, 256), BF16),
        pltpu.VMEM((count, 128, 128), F32),
        pltpu.VMEM((2, 32, 128, 128), F32),
        pltpu.VMEM((2, 32, 128, 128), F32),
        pltpu.VMEM((2, 32, 128, 128), F32),
        pltpu.VMEM((2, 2, 2, 2, 128, 128), F32),
        pltpu.VMEM((2, 2, 2, 4, 128, 128), F32),
        pltpu.VMEM((2, 4, 128, 128), F32),
        pltpu.VMEM((2, 2, 2, 2, 128, 128), F32),
        pltpu.VMEM((2, 2, 2, 4, 128, 128), F32),
        pltpu.VMEM((2, 4, 128, 128), F32),
        pltpu.VMEM((256, 256), F32),
        pltpu.VMEM((4, 128, 256), F32),
        pltpu.VMEM((4, 128, 256), F32),
        pltpu.VMEM((4, 128, 256), F32),
        pltpu.VMEM((4, 128, 256), F32),
        pltpu.VMEM((256, 256), F32),
        pltpu.VMEM((128, 256), F32),
        pltpu.VMEM((8, 16, 256), F32),
        pltpu.VMEM((8, 16, 256), F32),
        pltpu.VMEM((256, 256), F32),
        pltpu.VMEM((4, 256, 256), BF16),
        pltpu.VMEM((2, 8, 128), jnp.int32),
        pltpu.VMEM((16, 128), jnp.int32),
        pltpu.SMEM((16, 128), jnp.int32),
        pltpu.SemaphoreType.DMA((N_SEM,)),
        pltpu.SemaphoreType.DMA((N_SEM,)),
        pltpu.SemaphoreType.DMA((16,)),
    ]
    made = pl.pallas_call(
        lambda *refs: kernel(total_nodes, *refs),
        out_shape=out,
        in_specs=[any_, any_, any_, vmem, vmem, any_],
        out_specs=[any_] * 3,
        scratch_shapes=scratch,
        compiler_params=pltpu.CompilerParams(
            collective_id=0, has_side_effects=True, vmem_limit_bytes=63 * 1024 * 1024
        ),
        name="graph_layer",
    )(
        features.reshape(4, 128, width),
        weight_matrix,
        cotangent.reshape(4, 128, width),
        block_rows[0],
        block_cols[0],
        blocks[0, 0],
    )
    hidden, weight_grad, feature_grad = pl.pallas_call(
        hand_over,
        out_shape=out,
        in_specs=[any_] * 3,
        out_specs=[any_] * 3,
        scratch_shapes=[pltpu.VMEM(a.shape, F32) for a in out] + [pltpu.SemaphoreType.DMA((3,))] * 2,
        name="hand_over",
    )(*made)
    return hidden.reshape(rows_dev, width), weight_grad, feature_grad.reshape(rows_dev, width)


def solution(mesh):
    in_specs = (
        P(("col", "row"), None),
        P(),
        P(("row", "col"), None),
        P("row", "col", None),
        P("row", "col", None),
        P("row", "col", None, None, None),
    )
    out_specs = (P(("row", "col"), None), P(), P(("col", "row"), None))
    return jax.shard_map(shards, mesh=mesh, in_specs=in_specs, out_specs=out_specs, check_vma=False)
```

```python
import math
import jax
import jax.numpy as jnp
from jax import lax
from jax.experimental import pallas as pl
from jax.experimental.pallas import tpu as pltpu
from jax.sharding import PartitionSpec as P

F32 = jnp.float32
BF16 = jnp.bfloat16
MESH = pl.DeviceIdType.MESH
HA = 0
HB = 2
N_SEM = 192
FAR = 1 << 20


def split(value):
    high = value.astype(BF16)
    return high, (value - high.astype(F32)).astype(BF16)


def dot(a, b):
    return jnp.dot(a, b, preferred_element_type=F32)


def dot3(ah, al, bh, bl):
    return dot(ah, bh) + dot(al, bh) + dot(ah, bl)


def sort_tables(ids, table, base, scratch, other, sources):
    count = ids.shape[-1]
    scratch[...] = jnp.full(scratch.shape, FAR, jnp.int32)
    scratch[0:1, 0:count] = ids
    scratch[1:2, 0:count] = other
    lane_ids = jnp.broadcast_to(scratch[0:1, :], (128, 128))
    lane_other = jnp.broadcast_to(scratch[1:2, :], (128, 128))
    sub_ids, sub_other = lane_ids.T, lane_other.T
    lane = lax.broadcasted_iota(jnp.int32, (128, 128), 1)
    sub = lax.broadcasted_iota(jnp.int32, (128, 128), 0)

    def total(mask, value, axis):
        return jnp.sum(jnp.where(mask, value, 0), axis=axis, keepdims=True)

    rank = total((lane_ids < sub_ids) | ((lane_ids == sub_ids) & (lane < sub)), 1, 1)
    below = total(lane_ids < sub_ids, 1, 1)
    here = (jnp.broadcast_to(rank, (128, 128)) == lane) & (sub < count)
    order = total(here, sub, 0)
    source = total(here, sub_other, 0)
    starts = total(here, jnp.broadcast_to(below, (128, 128)), 0)
    upto = total(sub_ids <= lane, 1, 0)
    same = total(sub_ids == lane, 1, 0)
    table[base : base + 1, :] = jnp.clip(order, 0, count - 1)
    table[base + 1 : base + 2, :] = jnp.clip(source, 0, sources - 1)
    table[base + 2 : base + 3, :] = jnp.where(starts == lane[0:1, :], 1, 0)
    table[base + 3 : base + 4, :] = jnp.clip(upto - 1, 0, count - 1)
    table[base + 4 : base + 5, :] = jnp.where(same > 0, 1, 0)


class Links:
    def __init__(self, send_sem, recv_sem):
        self.send_sem, self.recv_sem, self.used, self.open = send_sem, recv_sem, 0, []

    def send(self, src, dst, device):
        i = self.used
        self.used += 1
        assert i < N_SEM
        copy = pltpu.make_async_remote_copy(
            src_ref=src, dst_ref=dst, send_sem=self.send_sem.at[i], recv_sem=self.recv_sem.at[i],
            device_id=device, device_id_type=MESH)
        copy.start()
        self.open.append(copy)
        return copy

    def flush(self):
        for copy in self.open:
            copy.wait_send()
        self.open = []


class GatherRing:
    def __init__(self, links, view, pos, plus, minus, size, cross=None):
        self.links, self.view, self.pos, self.plus, self.minus = links, view, pos, plus, minus
        self.half, self.cross = size // 2, cross
        self.left, self.right, self.across = lax.rem(pos + 3, 4), lax.rem(pos + 1, 4), lax.rem(pos + 2, 4)

    def pieces(self, pos):
        return self.view(pos, 0, self.half), self.view(pos, self.half, self.half)

    def start(self):
        send = self.links.send
        a, b = self.pieces(self.pos)
        self.c1 = send(a, a, self.plus)
        self.c2 = send(b, b, self.minus)
        self.c3 = send(b, b, self.plus)
        self.c4 = send(a, a, self.minus)

    def relay(self):
        send = self.links.send
        self.c1.wait_recv()
        a = self.pieces(self.left)[0]
        self.r1 = send(a, a, self.plus)
        self.c2.wait_recv()
        b = self.pieces(self.right)[1]
        self.r2 = send(b, b, self.minus)
        if self.cross:
            self.crossed = [send(b, b, self.cross)]

    def cross_left(self):
        self.c3.wait_recv()
        b = self.pieces(self.left)[1]
        self.crossed.append(self.links.send(b, b, self.cross))

    def cross_far(self):
        self.r2.wait_recv()
        b = self.pieces(self.across)[1]
        self.crossed.append(self.links.send(b, b, self.cross))

    def finish(self, arrived=None, crossed=()):
        if not self.cross:
            self.c3.wait_recv()
            self.r2.wait_recv()
        self.c4.wait_recv()
        self.r1.wait_recv()
        for copy in crossed:
            copy.wait_recv()
        if arrived:
            for pos in (self.left, self.right, self.across):
                arrived(self.view(pos, HA, 4))


class SumRing:
    def __init__(self, links, view, near, far, pos, plus, minus):
        self.links, self.view, self.near, self.far = links, view, near, far
        self.pos, self.plus, self.minus = pos, plus, minus

    def start(self):
        view, q, send = self.view, self.pos, self.links.send
        left, right, across = lax.rem(q + 3, 4), lax.rem(q + 1, 4), lax.rem(q + 2, 4)
        self.o1 = send(view(across, HA, 2), self.near.at[0], self.plus)
        self.o2 = send(view(across, HB, 2), self.near.at[1], self.minus)
        self.n1 = send(view(right, HB, 2), self.far.at[0, 2:4], self.plus)
        self.n2 = send(view(left, HA, 2), self.far.at[1, 0:2], self.minus)

    def relay(self):
        view, q, send = self.view, self.pos, self.links.send
        left, right = lax.rem(q + 3, 4), lax.rem(q + 1, 4)
        self.o1.wait_recv()
        part = view(right, HA, 2)
        part[...] += self.near[0]
        self.m1 = send(part, self.far.at[0, 0:2], self.plus)
        self.o2.wait_recv()
        part = view(left, HB, 2)
        part[...] += self.near[1]
        self.m2 = send(part, self.far.at[1, 2:4], self.minus)

    def finish(self):
        self.n1.wait_recv()
        self.n2.wait_recv()
        self.m1.wait_recv()
        self.m2.wait_recv()
        part = self.view(self.pos, HA, 4)
        part[...] += self.far[0] + self.far[1]
        return part


def kernel(total_nodes, feats, weight, cot, rows_in, cols_in, blocks, hidden_out, wgrad_out, fgrad_out,
           X, XX, A, AT, PS, OUT, BK, DR, CN, CF, CX, RN, RF, RX, W_ref, C_ref, AG, DP, HID, G, WH, WR, WS, WO,
           WP, IDS, TAB, TABS, send_sem, recv_sem, load_sem):
    row, col = lax.axis_index("row"), lax.axis_index("col")
    y, x_lo, core = row // 4, lax.rem(row // 2, 2), lax.rem(row, 2)
    z, x_hi = col // 2, lax.rem(col, 2)
    chip = row // 2

    def at_row(yy, xx, cc):
        return (yy * 4 + xx * 2 + cc, col)

    def at_col(zz, xx):
        return (row, zz * 2 + xx)

    y_plus, y_minus = at_row(lax.rem(y + 1, 4), x_lo, core), at_row(lax.rem(y + 3, 4), x_lo, core)
    z_plus, z_minus = at_col(lax.rem(z + 1, 4), x_hi), at_col(lax.rem(z + 3, 4), x_hi)
    x_near, twin, x_far = at_row(y, 1 - x_lo, core), at_row(y, x_lo, 1 - core), at_col(z, 1 - x_hi)
    col_peers = [(row, lax.rem(col + j, 8)) for j in range(1, 8)]
    row_peers = [(lax.rem(chip + j, 8) * 2 + core, col) for j in range(1, 8)]

    loads = []

    def load(src, dst):
        copy = pltpu.make_async_copy(src, dst, load_sem.at[len(loads)])
        copy.start()
        loads.append(copy)
        return copy

    lanes = [pl.ds(f * 128, 128) for f in range(2)]
    mine_x = [X.at[f, pl.ds(row * 4, 4)] for f in range(2)]
    get_x = [load(feats.at[:, :, lanes[f]], mine_x[f]) for f in range(2)]
    get_a = load(blocks, PS)
    get_w = load(weight, W_ref)
    get_c = load(cot, C_ref)

    barrier = pltpu.get_barrier_semaphore()
    peers = col_peers + row_peers + [twin]
    for peer in peers:
        pl.semaphore_signal(barrier, inc=1, device_id=peer, device_id_type=MESH)
    pl.semaphore_wait(barrier, len(peers))

    links = Links(send_sem, recv_sem)
    send = links.send

    def x_view(f, xx):
        return lambda q, half, n: X.at[f, pl.ds((q * 4 + xx * 2 + core) * 4 + half, n)]

    own = [GatherRing(links, x_view(f, x_lo), y, y_plus, y_minus, 4, x_near) for f in range(2)]
    other = [GatherRing(links, x_view(f, 1 - x_lo), y, y_plus, y_minus, 2) for f in range(2)]
    xs, twins = [None, None], [[], []]

    def to_twin(f):
        return lambda piece: twins[f].append(send(piece, piece, twin))

    def across(view, pos, device):
        return [send(view(pos, half, 2), view(pos, half, 2), device) for half in (HA, HB)]

    get_x[0].wait()
    xs[0] = across(x_view(0, x_lo), y, x_near)
    own[0].start()
    get_x[1].wait()
    to_twin(0)(mine_x[0])
    to_twin(1)(mine_x[1])

    sort_tables(rows_in[...], TAB, 0, IDS.at[0], cols_in[...], 64)
    sort_tables(cols_in[...], TAB, 8, IDS.at[1], rows_in[...], 32)
    get_tab = load(TAB, TABS)
    get_tab.wait()
    get_a.wait()

    def prepare(k, carry):
        value = PS[k]
        high, low = split(value)
        A[k, :, 0:128] = high
        A[k, :, 128:256] = low
        high, low = split(value.T)
        AT[k, :, 0:128] = high
        AT[k, :, 128:256] = low
        return carry

    own[0].relay()
    xs[0][0].wait_recv()
    other[0].start()
    lax.fori_loop(0, 16, prepare, 0)
    own[0].cross_left()
    xs[0][1].wait_recv()
    to_twin(0)(x_view(0, 1 - x_lo)(y, HA, 4))
    lax.fori_loop(16, 48, prepare, 0)
    other[0].relay()
    own[0].cross_far()
    own[1].start()
    xs[1] = across(x_view(1, x_lo), y, x_near)
    lax.fori_loop(48, 96, prepare, 0)
    get_w.wait()
    high, low = split(W_ref[...])
    WP[0], WP[1] = high, low
    high, low = split(W_ref[...].T)
    WP[2], WP[3] = high, low
    get_c.wait()

    def to_pairs(source, f, count):
        def step(k, carry):
            high, low = split(source[f, k])
            XX[k, :, 0:128] = high
            XX[k, :, 128:256] = low
            return carry

        lax.fori_loop(0, count, step, 0, unroll=2)

    def tile_product(left, base, between=None):
        def step(p, total):
            lhs = left[TABS[base, p]]
            pair = XX[TABS[base + 1, p]]
            result = dot(lhs, jnp.concatenate([pair, pair], axis=0))
            term = result[:, 0:128] + result[:, 128:256]
            total = jnp.where(TABS[base + 2, p] == 1, term, total + term)
            PS[p] = total
            return total

        middle = PS.shape[0] // 2
        total = lax.fori_loop(0, middle, step, jnp.zeros((128, 128), F32), unroll=4)
        if between:
            between()
        lax.fori_loop(middle, PS.shape[0], step, total, unroll=4)

    def collect(dst, f, base, start, count, place):
        def step(r, carry):
            t = place(r)
            dst[f, t] = jnp.where(TABS[base + 4, t] == 1, PS[TABS[base + 3, t]], 0.0)
            return carry

        lax.fori_loop(start, start + count, step, 0, unroll=2)

    def same(r):
        return r

    def col_view(f, xx):
        return lambda q, half, n: OUT.at[f, pl.ds((q * 2 + xx) * 4 + half, n)]

    col_far = [SumRing(links, col_view(f, 1 - x_hi), CN.at[f, 0], CF.at[f, 0], z, z_plus, z_minus) for f in range(2)]
    col_own = [SumRing(links, col_view(f, x_hi), CN.at[f, 1], CF.at[f, 1], z, z_plus, z_minus) for f in range(2)]

    def finish_gather(f):
        own[f].finish(to_twin(f))
        other[f].finish(to_twin(f), own[f].crossed)
        for copy in twins[f]:
            copy.wait_recv()

    def forward(f, between=None):
        to_pairs(X, f, X.shape[1])
        tile_product(A, 0, between)
        collect(OUT, f, 0, 0, OUT.shape[1], same)
        col_far[f].start()

    def next_half():
        own[1].relay()
        xs[1][0].wait_recv()
        other[1].start()

    finish_gather(0)
    forward(0, next_half)
    own[1].cross_left()
    xs[1][1].wait_recv()
    to_twin(1)(x_view(1, 1 - x_lo)(y, HA, 4))
    other[1].relay()
    own[1].cross_far()
    col_far[0].relay()
    col_own[0].start()
    finish_gather(1)
    sums = [send(col_far[0].finish(), CX.at[0], x_far)]
    col_own[0].relay()
    forward(1)
    col_own[0].finish()
    col_far[1].relay()
    col_own[1].start()
    sums.append(send(col_far[1].finish(), CX.at[1], x_far))
    col_own[1].relay()
    col_own[1].finish()
    for f in range(2):
        sums[f].wait_recv()

    early, links.open = links.open, []

    def middle(i, carry):
        agg0 = OUT[0, col * 4 + i] + CX[0, i]
        agg1 = OUT[1, col * 4 + i] + CX[1, i]
        agg = jnp.concatenate([agg0, agg1], axis=1)
        ah, al = split(agg)
        pre = dot3(ah, al, WP[0], WP[1])
        sig = 1.0 / (1.0 + jnp.exp(-pre))
        HID[i] = pre * sig
        dpre = C_ref[i] * sig * (1.0 + pre * (1.0 - sig))
        dh, dl = split(dpre)
        back = dot3(dh, dl, WP[2], WP[3])
        BK[0, col * 4 + i] = back[:, 0:128]
        BK[1, col * 4 + i] = back[:, 128:256]
        AG[i] = agg
        DP[i] = dpre
        return carry

    lax.fori_loop(0, 4, middle, 0)

    def b_view(f, xx):
        return lambda q, half, n: BK.at[f, pl.ds((q * 2 + xx) * 4 + half, n)]

    own = [GatherRing(links, b_view(f, x_hi), z, z_plus, z_minus, 4, x_far) for f in range(2)]
    other = [GatherRing(links, b_view(f, 1 - x_hi), z, z_plus, z_minus, 2) for f in range(2)]
    xs = [across(b_view(0, x_hi), z, x_far)]
    own[0].start()
    put_h = load(HID, hidden_out)

    def term(i, total):
        th, tl = split(AG[i].T)
        dh, dl = split(DP[i])
        return total + dot3(th, tl, dh, dl)

    G[...] = lax.fori_loop(0, 4, term, jnp.zeros(G.shape, F32)) / jnp.float32(math.sqrt(total_nodes))
    half_of = lambda c: pl.ds(pl.multiple_of(c * 128, 128), 128)
    w1 = send(G.at[half_of(1 - core)], WH, twin)

    own[0].relay()
    xs[0][0].wait_recv()
    other[0].start()
    w1.wait_recv()
    WH[...] += G[half_of(core), :]
    slot = lambda m: pl.ds(pl.multiple_of(m * 16, 16), 16)
    w2 = [send(WH.at[slot(peer[1])], WR.at[col], peer) for peer in col_peers]
    WR[col] = WH[slot(col), :]
    own[0].cross_left()
    other[0].relay()
    own[0].cross_far()
    own[1].start()
    xs.append(across(b_view(1, x_hi), z, x_far))
    for copy in w2:
        copy.wait_recv()

    def add_all(parts):
        total = parts[0]
        for m in range(1, 8):
            total = total + parts[m]
        return total

    WS[chip] = add_all(WR)
    w3 = [send(WS.at[chip], WS.at[chip], peer) for peer in row_peers]

    def r_view(f, xx, cc):
        return lambda q, half, n: X.at[f, pl.ds((q * 4 + xx * 2 + cc) * 4 + half, n)]

    def part(xx, cc):
        return lambda r: ((r // 4) * 4 + xx * 2 + cc) * 4 + lax.rem(r, 4)

    row_far = [SumRing(links, r_view(f, 1 - x_lo, core), RN.at[f, 0], RF.at[f, 0], y, y_plus, y_minus) for f in range(2)]
    row_own = [SumRing(links, r_view(f, x_lo, core), RN.at[f, 1], RF.at[f, 1], y, y_plus, y_minus) for f in range(2)]

    def finish_back(f):
        own[f].finish()
        xs[f][1].wait_recv()
        other[f].finish(None, own[f].crossed)

    for copy in early:
        copy.wait_send()

    def backward(f, between=None):
        to_pairs(BK, f, BK.shape[1])
        tile_product(AT, 8, between)

        moves = []
        for k, xx in enumerate((1 - x_lo, x_lo)):
            collect(X, f, 8, 0, 16, part(xx, 1 - core))
            for m in range(4):
                moves.append(send(r_view(f, xx, 1 - core)(m, HA, 4), DR.at[f, pl.ds(k * 16 + m * 4, 4)], twin))
        for xx in (1 - x_lo, x_lo):
            collect(X, f, 8, 0, 16, part(xx, core))
        return moves

    def join(f, moves, k):
        for copy in moves[k * 4 : k * 4 + 4]:
            copy.wait_recv()
        place = part(x_lo if k else 1 - x_lo, core)

        def step(r, carry):
            X[f, place(r)] += DR[f, k * 16 + r]
            return carry

        lax.fori_loop(0, 16, step, 0, unroll=2)

    finish_back(0)
    moves = backward(0, next_half)
    own[1].cross_left()
    join(0, moves, 0)
    row_far[0].start()
    other[1].relay()
    own[1].cross_far()
    join(0, moves, 1)
    for copy in w3:
        copy.wait_recv()
    mine_w = WO.at[pl.ds(pl.multiple_of(core * 128 + col * 16, 16), 16)]
    mine_w[...] = add_all(WS)
    w4 = [send(mine_w, mine_w, peer) for peer in col_peers]
    row_far[0].relay()
    row_own[0].start()
    finish_back(1)
    moves = backward(1)
    row_own[0].relay()
    sums = [send(row_far[0].finish(), RX.at[0], x_near)]
    join(1, moves, 0)
    row_far[1].start()
    join(1, moves, 1)
    for copy in w4:
        copy.wait_recv()
    w5 = send(WO.at[half_of(core)], WO.at[half_of(core)], twin)
    row_own[0].finish()
    row_far[1].relay()
    row_own[1].start()
    w5.wait_recv()
    put_w = load(WO, wgrad_out)
    sums[0].wait_recv()
    mine_x[0][...] += RX[0]
    put_0 = load(mine_x[0], fgrad_out.at[:, :, lanes[0]])
    sums.append(send(row_far[1].finish(), RX.at[1], x_near))
    row_own[1].relay()
    row_own[1].finish()
    sums[1].wait_recv()
    mine_x[1][...] += RX[1]
    put_1 = load(mine_x[1], fgrad_out.at[:, :, lanes[1]])
    links.flush()
    for copy in (put_h, put_w, put_0, put_1):
        copy.wait()


def hand_over(*refs):
    count = len(refs) // 3
    sources, results, held = refs[:count], refs[count : 2 * count], refs[2 * count : 3 * count]
    in_sem, out_sem = refs[3 * count :]
    ins = [pltpu.make_async_copy(sources[i], held[i], in_sem.at[i]) for i in range(count)]
    outs = [pltpu.make_async_copy(held[i], results[i], out_sem.at[i]) for i in range(count)]
    for copy in ins:
        copy.start()
    for i in range(count):
        ins[i].wait()
        outs[i].start()
    for copy in outs:
        copy.wait()


def shards(features, weight_matrix, cotangent, block_rows, block_cols, blocks):
    assert lax.axis_size("row") == 16 and lax.axis_size("col") == 8
    count = blocks.shape[2]
    rows_dev, width = features.shape
    assert (rows_dev, width) == (512, 256) and blocks.shape[3] == 128 and count <= 128
    total_nodes = rows_dev * 128
    any_ = pl.BlockSpec(memory_space=pl.ANY)
    vmem = pl.BlockSpec(memory_space=pltpu.VMEM)
    out = [
        jax.ShapeDtypeStruct((4, 128, 256), F32),
        jax.ShapeDtypeStruct((256, 256), F32),
        jax.ShapeDtypeStruct((4, 128, 256), F32),
    ]
    scratch = [
        pltpu.VMEM((2, 64, 128, 128), F32),
        pltpu.VMEM((64, 128, 256), BF16),
        pltpu.VMEM((count, 128, 256), BF16),
        pltpu.VMEM((count, 128, 256), BF16),
        pltpu.VMEM((count, 128, 128), F32),
        pltpu.VMEM((2, 32, 128, 128), F32),
        pltpu.VMEM((2, 32, 128, 128), F32),
        pltpu.VMEM((2, 32, 128, 128), F32),
        pltpu.VMEM((2, 2, 2, 2, 128, 128), F32),
        pltpu.VMEM((2, 2, 2, 4, 128, 128), F32),
        pltpu.VMEM((2, 4, 128, 128), F32),
        pltpu.VMEM((2, 2, 2, 2, 128, 128), F32),
        pltpu.VMEM((2, 2, 2, 4, 128, 128), F32),
        pltpu.VMEM((2, 4, 128, 128), F32),
        pltpu.VMEM((256, 256), F32),
        pltpu.VMEM((4, 128, 256), F32),
        pltpu.VMEM((4, 128, 256), F32),
        pltpu.VMEM((4, 128, 256), F32),
        pltpu.VMEM((4, 128, 256), F32),
        pltpu.VMEM((256, 256), F32),
        pltpu.VMEM((128, 256), F32),
        pltpu.VMEM((8, 16, 256), F32),
        pltpu.VMEM((8, 16, 256), F32),
        pltpu.VMEM((256, 256), F32),
        pltpu.VMEM((4, 256, 256), BF16),
        pltpu.VMEM((2, 8, 128), jnp.int32),
        pltpu.VMEM((16, 128), jnp.int32),
        pltpu.SMEM((16, 128), jnp.int32),
        pltpu.SemaphoreType.DMA((N_SEM,)),
        pltpu.SemaphoreType.DMA((N_SEM,)),
        pltpu.SemaphoreType.DMA((16,)),
    ]
    made = pl.pallas_call(
        lambda *refs: kernel(total_nodes, *refs),
        out_shape=out,
        in_specs=[any_, any_, any_, vmem, vmem, any_],
        out_specs=[any_] * 3,
        scratch_shapes=scratch,
        compiler_params=pltpu.CompilerParams(
            collective_id=0, has_side_effects=True, vmem_limit_bytes=63 * 1024 * 1024
        ),
        name="graph_layer",
    )(
        features.reshape(4, 128, width),
        weight_matrix,
        cotangent.reshape(4, 128, width),
        block_rows[0],
        block_cols[0],
        blocks[0, 0],
    )
    hidden, weight_grad, feature_grad = pl.pallas_call(
        hand_over,
        out_shape=out,
        in_specs=[any_] * 3,
        out_specs=[any_] * 3,
        scratch_shapes=[pltpu.VMEM(a.shape, F32) for a in out] + [pltpu.SemaphoreType.DMA((3,))] * 2,
        name="hand_over",
    )(*made)
    return hidden.reshape(rows_dev, width), weight_grad, feature_grad.reshape(rows_dev, width)


def solution(mesh):
    in_specs = (
        P(("col", "row"), None),
        P(),
        P(("row", "col"), None),
        P("row", "col", None),
        P("row", "col", None),
        P("row", "col", None, None, None),
    )
    out_specs = (P(("row", "col"), None), P(), P(("col", "row"), None))
    return jax.shard_map(shards, mesh=mesh, in_specs=in_specs, out_specs=out_specs, check_vma=False)
```

```python
import math
import jax
import jax.numpy as jnp
from jax import lax
from jax.experimental import pallas as pl
from jax.experimental.pallas import tpu as pltpu
from jax.sharding import PartitionSpec as P

F32 = jnp.float32
BF16 = jnp.bfloat16
MESH = pl.DeviceIdType.MESH
HA = 0
HB = 2
N_SEM = 192
FAR = 1 << 20


def split(value):
    high = value.astype(BF16)
    return high, (value - high.astype(F32)).astype(BF16)


def dot(a, b):
    return jnp.dot(a, b, preferred_element_type=F32)


def dot3(ah, al, bh, bl):
    return dot(ah, bh) + dot(al, bh) + dot(ah, bl)


def sort_tables(ids, table, base, scratch, other, sources):
    count = ids.shape[-1]
    scratch[...] = jnp.full(scratch.shape, FAR, jnp.int32)
    scratch[0:1, 0:count] = ids
    scratch[1:2, 0:count] = other
    lane_ids = jnp.broadcast_to(scratch[0:1, :], (128, 128))
    lane_other = jnp.broadcast_to(scratch[1:2, :], (128, 128))
    sub_ids, sub_other = lane_ids.T, lane_other.T
    lane = lax.broadcasted_iota(jnp.int32, (128, 128), 1)
    sub = lax.broadcasted_iota(jnp.int32, (128, 128), 0)

    def total(mask, value, axis):
        return jnp.sum(jnp.where(mask, value, 0), axis=axis, keepdims=True)

    rank = total((lane_ids < sub_ids) | ((lane_ids == sub_ids) & (lane < sub)), 1, 1)
    below = total(lane_ids < sub_ids, 1, 1)
    here = (jnp.broadcast_to(rank, (128, 128)) == lane) & (sub < count)
    order = total(here, sub, 0)
    source = total(here, sub_other, 0)
    starts = total(here, jnp.broadcast_to(below, (128, 128)), 0)
    upto = total(sub_ids <= lane, 1, 0)
    same = total(sub_ids == lane, 1, 0)
    table[base : base + 1, :] = jnp.clip(order, 0, count - 1)
    table[base + 1 : base + 2, :] = jnp.clip(source, 0, sources - 1)
    table[base + 2 : base + 3, :] = jnp.where(starts == lane[0:1, :], 1, 0)
    table[base + 3 : base + 4, :] = jnp.clip(upto - 1, 0, count - 1)
    table[base + 4 : base + 5, :] = jnp.where(same > 0, 1, 0)


class Links:
    def __init__(self, send_sem, recv_sem):
        self.send_sem, self.recv_sem, self.used, self.open = send_sem, recv_sem, 0, []

    def send(self, src, dst, device):
        i = self.used
        self.used += 1
        assert i < N_SEM
        copy = pltpu.make_async_remote_copy(
            src_ref=src, dst_ref=dst, send_sem=self.send_sem.at[i], recv_sem=self.recv_sem.at[i],
            device_id=device, device_id_type=MESH)
        copy.start()
        self.open.append(copy)
        return copy

    def flush(self):
        for copy in self.open:
            copy.wait_send()
        self.open = []


class GatherRing:
    def __init__(self, links, view, pos, plus, minus, size, cross=None):
        self.links, self.view, self.pos, self.plus, self.minus = links, view, pos, plus, minus
        self.half, self.cross = size // 2, cross
        self.left, self.right, self.across = lax.rem(pos + 3, 4), lax.rem(pos + 1, 4), lax.rem(pos + 2, 4)

    def pieces(self, pos):
        return self.view(pos, 0, self.half), self.view(pos, self.half, self.half)

    def start(self):
        send = self.links.send
        a, b = self.pieces(self.pos)
        self.c1 = send(a, a, self.plus)
        self.c2 = send(b, b, self.minus)
        self.c3 = send(b, b, self.plus)
        self.c4 = send(a, a, self.minus)

    def relay(self):
        send = self.links.send
        self.c1.wait_recv()
        a = self.pieces(self.left)[0]
        self.r1 = send(a, a, self.plus)
        self.c2.wait_recv()
        b = self.pieces(self.right)[1]
        self.r2 = send(b, b, self.minus)
        if self.cross:
            self.crossed = [send(b, b, self.cross)]

    def cross_left(self):
        self.c3.wait_recv()
        b = self.pieces(self.left)[1]
        self.crossed.append(self.links.send(b, b, self.cross))

    def cross_far(self):
        self.r2.wait_recv()
        b = self.pieces(self.across)[1]
        self.crossed.append(self.links.send(b, b, self.cross))

    def finish(self, arrived=None, crossed=()):
        if not self.cross:
            self.c3.wait_recv()
            self.r2.wait_recv()
        self.c4.wait_recv()
        self.r1.wait_recv()
        for copy in crossed:
            copy.wait_recv()
        if arrived:
            for pos in (self.left, self.right, self.across):
                arrived(self.view(pos, HA, 4))


class SumRing:
    def __init__(self, links, view, near, far, pos, plus, minus):
        self.links, self.view, self.near, self.far = links, view, near, far
        self.pos, self.plus, self.minus = pos, plus, minus

    def start(self):
        view, q, send = self.view, self.pos, self.links.send
        left, right, across = lax.rem(q + 3, 4), lax.rem(q + 1, 4), lax.rem(q + 2, 4)
        self.o1 = send(view(across, HA, 2), self.near.at[0], self.plus)
        self.o2 = send(view(across, HB, 2), self.near.at[1], self.minus)
        self.n1 = send(view(right, HB, 2), self.far.at[0, 2:4], self.plus)
        self.n2 = send(view(left, HA, 2), self.far.at[1, 0:2], self.minus)

    def relay(self):
        view, q, send = self.view, self.pos, self.links.send
        left, right = lax.rem(q + 3, 4), lax.rem(q + 1, 4)
        self.o1.wait_recv()
        part = view(right, HA, 2)
        part[...] += self.near[0]
        self.m1 = send(part, self.far.at[0, 0:2], self.plus)
        self.o2.wait_recv()
        part = view(left, HB, 2)
        part[...] += self.near[1]
        self.m2 = send(part, self.far.at[1, 2:4], self.minus)

    def finish(self):
        self.n1.wait_recv()
        self.n2.wait_recv()
        self.m1.wait_recv()
        self.m2.wait_recv()
        part = self.view(self.pos, HA, 4)
        part[...] += self.far[0] + self.far[1]
        return part


def kernel(total_nodes, feats, weight, cot, rows_in, cols_in, blocks, hidden_out, wgrad_out, fgrad_out,
           X, XX, A, AT, PS, OUT, BK, DR, CN, CF, CX, RN, RF, RX, W_ref, C_ref, AG, DP, HID, G, WH, WR, WS, WO,
           WP, IDS, TAB, TABS, send_sem, recv_sem, load_sem):
    row, col = lax.axis_index("row"), lax.axis_index("col")
    y, x_lo, core = row // 4, lax.rem(row // 2, 2), lax.rem(row, 2)
    z, x_hi = col // 2, lax.rem(col, 2)
    chip = row // 2

    def at_row(yy, xx, cc):
        return (yy * 4 + xx * 2 + cc, col)

    def at_col(zz, xx):
        return (row, zz * 2 + xx)

    y_plus, y_minus = at_row(lax.rem(y + 1, 4), x_lo, core), at_row(lax.rem(y + 3, 4), x_lo, core)
    z_plus, z_minus = at_col(lax.rem(z + 1, 4), x_hi), at_col(lax.rem(z + 3, 4), x_hi)
    x_near, twin, x_far = at_row(y, 1 - x_lo, core), at_row(y, x_lo, 1 - core), at_col(z, 1 - x_hi)
    col_peers = [(row, lax.rem(col + j, 8)) for j in range(1, 8)]
    row_peers = [(lax.rem(chip + j, 8) * 2 + core, col) for j in range(1, 8)]

    loads = []

    def load(src, dst):
        copy = pltpu.make_async_copy(src, dst, load_sem.at[len(loads)])
        copy.start()
        loads.append(copy)
        return copy

    lanes = [pl.ds(f * 128, 128) for f in range(2)]
    mine_x = [X.at[f, pl.ds(row * 4, 4)] for f in range(2)]
    get_x = [load(feats.at[:, :, lanes[f]], mine_x[f]) for f in range(2)]
    get_a = load(blocks, PS)
    get_w = load(weight, W_ref)
    get_c = load(cot, C_ref)

    barrier = pltpu.get_barrier_semaphore()
    peers = col_peers + row_peers + [twin]
    for peer in peers:
        pl.semaphore_signal(barrier, inc=1, device_id=peer, device_id_type=MESH)
    pl.semaphore_wait(barrier, len(peers))

    links = Links(send_sem, recv_sem)
    send = links.send

    def x_view(f, xx):
        return lambda q, half, n: X.at[f, pl.ds((q * 4 + xx * 2 + core) * 4 + half, n)]

    own = [GatherRing(links, x_view(f, x_lo), y, y_plus, y_minus, 4, x_near) for f in range(2)]
    other = [GatherRing(links, x_view(f, 1 - x_lo), y, y_plus, y_minus, 2) for f in range(2)]
    xs, twins = [None, None], [[], []]

    def to_twin(f):
        return lambda piece: twins[f].append(send(piece, piece, twin))

    def across(view, pos, device):
        return [send(view(pos, half, 2), view(pos, half, 2), device) for half in (HA, HB)]

    get_x[0].wait()
    xs[0] = across(x_view(0, x_lo), y, x_near)
    own[0].start()
    get_x[1].wait()
    to_twin(0)(mine_x[0])
    to_twin(1)(mine_x[1])

    sort_tables(rows_in[...], TAB, 0, IDS.at[0], cols_in[...], 64)
    sort_tables(cols_in[...], TAB, 8, IDS.at[1], rows_in[...], 32)
    get_tab = load(TAB, TABS)
    get_tab.wait()
    get_a.wait()

    def prepare(k, carry):
        value = PS[k]
        high, low = split(value)
        A[k, :, 0:128] = high
        A[k, :, 128:256] = low
        high, low = split(value.T)
        AT[k, :, 0:128] = high
        AT[k, :, 128:256] = low
        return carry

    own[0].relay()
    xs[0][0].wait_recv()
    other[0].start()
    lax.fori_loop(0, 16, prepare, 0, unroll=2)
    own[0].cross_left()
    xs[0][1].wait_recv()
    to_twin(0)(x_view(0, 1 - x_lo)(y, HA, 4))
    lax.fori_loop(16, 48, prepare, 0, unroll=2)
    other[0].relay()
    own[0].cross_far()
    own[1].start()
    xs[1] = across(x_view(1, x_lo), y, x_near)
    lax.fori_loop(48, 96, prepare, 0, unroll=2)
    get_w.wait()
    high, low = split(W_ref[...])
    WP[0], WP[1] = high, low
    high, low = split(W_ref[...].T)
    WP[2], WP[3] = high, low
    get_c.wait()

    def to_pairs(source, f, count):
        def step(k, carry):
            high, low = split(source[f, k])
            XX[k, :, 0:128] = high
            XX[k, :, 128:256] = low
            return carry

        lax.fori_loop(0, count, step, 0, unroll=4)

    def tile_product(left, base, between=None):
        def step(p, total):
            lhs = left[TABS[base, p]]
            pair = XX[TABS[base + 1, p]]
            result = dot(lhs, jnp.concatenate([pair, pair], axis=0))
            term = result[:, 0:128] + result[:, 128:256]
            total = jnp.where(TABS[base + 2, p] == 1, term, total + term)
            PS[p] = total
            return total

        middle = PS.shape[0] // 2
        total = lax.fori_loop(0, middle, step, jnp.zeros((128, 128), F32), unroll=16)
        if between:
            between()
        lax.fori_loop(middle, PS.shape[0], step, total, unroll=16)

    def collect(dst, f, base, start, count, place):
        def step(r, carry):
            t = place(r)
            dst[f, t] = jnp.where(TABS[base + 4, t] == 1, PS[TABS[base + 3, t]], 0.0)
            return carry

        lax.fori_loop(start, start + count, step, 0, unroll=4)

    def same(r):
        return r

    def col_view(f, xx):
        return lambda q, half, n: OUT.at[f, pl.ds((q * 2 + xx) * 4 + half, n)]

    col_far = [SumRing(links, col_view(f, 1 - x_hi), CN.at[f, 0], CF.at[f, 0], z, z_plus, z_minus) for f in range(2)]
    col_own = [SumRing(links, col_view(f, x_hi), CN.at[f, 1], CF.at[f, 1], z, z_plus, z_minus) for f in range(2)]

    def finish_gather(f):
        own[f].finish(to_twin(f))
        other[f].finish(to_twin(f), own[f].crossed)
        for copy in twins[f]:
            copy.wait_recv()

    def forward(f, between=None):
        to_pairs(X, f, X.shape[1])
        tile_product(A, 0, between)
        collect(OUT, f, 0, 0, OUT.shape[1], same)
        col_far[f].start()

    def next_half():
        own[1].relay()
        xs[1][0].wait_recv()
        other[1].start()

    finish_gather(0)
    forward(0, next_half)
    own[1].cross_left()
    xs[1][1].wait_recv()
    to_twin(1)(x_view(1, 1 - x_lo)(y, HA, 4))
    other[1].relay()
    own[1].cross_far()
    col_far[0].relay()
    col_own[0].start()
    finish_gather(1)
    sums = [send(col_far[0].finish(), CX.at[0], x_far)]
    col_own[0].relay()
    forward(1)
    col_own[0].finish()
    col_far[1].relay()
    col_own[1].start()
    sums.append(send(col_far[1].finish(), CX.at[1], x_far))
    col_own[1].relay()
    col_own[1].finish()
    for f in range(2):
        sums[f].wait_recv()

    early, links.open = links.open, []

    def middle(i, carry):
        agg0 = OUT[0, col * 4 + i] + CX[0, i]
        agg1 = OUT[1, col * 4 + i] + CX[1, i]
        agg = jnp.concatenate([agg0, agg1], axis=1)
        ah, al = split(agg)
        pre = dot3(ah, al, WP[0], WP[1])
        sig = 1.0 / (1.0 + jnp.exp(-pre))
        HID[i] = pre * sig
        dpre = C_ref[i] * sig * (1.0 + pre * (1.0 - sig))
        dh, dl = split(dpre)
        back = dot3(dh, dl, WP[2], WP[3])
        BK[0, col * 4 + i] = back[:, 0:128]
        BK[1, col * 4 + i] = back[:, 128:256]
        AG[i] = agg
        DP[i] = dpre
        return carry

    lax.fori_loop(0, 4, middle, 0)

    def b_view(f, xx):
        return lambda q, half, n: BK.at[f, pl.ds((q * 2 + xx) * 4 + half, n)]

    own = [GatherRing(links, b_view(f, x_hi), z, z_plus, z_minus, 4, x_far) for f in range(2)]
    other = [GatherRing(links, b_view(f, 1 - x_hi), z, z_plus, z_minus, 2) for f in range(2)]
    xs = [across(b_view(0, x_hi), z, x_far)]
    own[0].start()
    put_h = load(HID, hidden_out)

    def term(i, total):
        th, tl = split(AG[i].T)
        dh, dl = split(DP[i])
        return total + dot3(th, tl, dh, dl)

    G[...] = lax.fori_loop(0, 4, term, jnp.zeros(G.shape, F32)) / jnp.float32(math.sqrt(total_nodes))
    half_of = lambda c: pl.ds(pl.multiple_of(c * 128, 128), 128)
    w1 = send(G.at[half_of(1 - core)], WH, twin)

    own[0].relay()
    xs[0][0].wait_recv()
    other[0].start()
    w1.wait_recv()
    WH[...] += G[half_of(core), :]
    slot = lambda m: pl.ds(pl.multiple_of(m * 16, 16), 16)
    w2 = [send(WH.at[slot(peer[1])], WR.at[col], peer) for peer in col_peers]
    WR[col] = WH[slot(col), :]
    own[0].cross_left()
    other[0].relay()
    own[0].cross_far()
    own[1].start()
    xs.append(across(b_view(1, x_hi), z, x_far))
    for copy in w2:
        copy.wait_recv()

    def add_all(parts):
        total = parts[0]
        for m in range(1, 8):
            total = total + parts[m]
        return total

    WS[chip] = add_all(WR)
    w3 = [send(WS.at[chip], WS.at[chip], peer) for peer in row_peers]

    def r_view(f, xx, cc):
        return lambda q, half, n: X.at[f, pl.ds((q * 4 + xx * 2 + cc) * 4 + half, n)]

    def part(xx, cc):
        return lambda r: ((r // 4) * 4 + xx * 2 + cc) * 4 + lax.rem(r, 4)

    row_far = [SumRing(links, r_view(f, 1 - x_lo, core), RN.at[f, 0], RF.at[f, 0], y, y_plus, y_minus) for f in range(2)]
    row_own = [SumRing(links, r_view(f, x_lo, core), RN.at[f, 1], RF.at[f, 1], y, y_plus, y_minus) for f in range(2)]

    def finish_back(f):
        own[f].finish()
        xs[f][1].wait_recv()
        other[f].finish(None, own[f].crossed)

    for copy in early:
        copy.wait_send()

    def backward(f, between=None):
        to_pairs(BK, f, BK.shape[1])
        tile_product(AT, 8, between)

        moves = []
        for k, xx in enumerate((1 - x_lo, x_lo)):
            collect(X, f, 8, 0, 16, part(xx, 1 - core))
            for m in range(4):
                moves.append(send(r_view(f, xx, 1 - core)(m, HA, 4), DR.at[f, pl.ds(k * 16 + m * 4, 4)], twin))
        for xx in (1 - x_lo, x_lo):
            collect(X, f, 8, 0, 16, part(xx, core))
        return moves

    def join(f, moves, k):
        for copy in moves[k * 4 : k * 4 + 4]:
            copy.wait_recv()
        place = part(x_lo if k else 1 - x_lo, core)

        def step(r, carry):
            X[f, place(r)] += DR[f, k * 16 + r]
            return carry

        lax.fori_loop(0, 16, step, 0, unroll=4)

    finish_back(0)
    moves = backward(0, next_half)
    own[1].cross_left()
    join(0, moves, 0)
    row_far[0].start()
    other[1].relay()
    own[1].cross_far()
    join(0, moves, 1)
    for copy in w3:
        copy.wait_recv()
    mine_w = WO.at[pl.ds(pl.multiple_of(core * 128 + col * 16, 16), 16)]
    mine_w[...] = add_all(WS)
    w4 = [send(mine_w, mine_w, peer) for peer in col_peers]
    row_far[0].relay()
    row_own[0].start()
    finish_back(1)
    moves = backward(1)
    row_own[0].relay()
    sums = [send(row_far[0].finish(), RX.at[0], x_near)]
    join(1, moves, 0)
    row_far[1].start()
    join(1, moves, 1)
    for copy in w4:
        copy.wait_recv()
    w5 = send(WO.at[half_of(core)], WO.at[half_of(core)], twin)
    row_own[0].finish()
    row_far[1].relay()
    row_own[1].start()
    w5.wait_recv()
    put_w = load(WO, wgrad_out)
    sums[0].wait_recv()
    mine_x[0][...] += RX[0]
    put_0 = load(mine_x[0], fgrad_out.at[:, :, lanes[0]])
    sums.append(send(row_far[1].finish(), RX.at[1], x_near))
    row_own[1].relay()
    row_own[1].finish()
    sums[1].wait_recv()
    mine_x[1][...] += RX[1]
    put_1 = load(mine_x[1], fgrad_out.at[:, :, lanes[1]])
    links.flush()
    for copy in (put_h, put_w, put_0, put_1):
        copy.wait()


def hand_over(*refs):
    count = len(refs) // 3
    sources, results, held = refs[:count], refs[count : 2 * count], refs[2 * count : 3 * count]
    in_sem, out_sem = refs[3 * count :]
    ins = [pltpu.make_async_copy(sources[i], held[i], in_sem.at[i]) for i in range(count)]
    outs = [pltpu.make_async_copy(held[i], results[i], out_sem.at[i]) for i in range(count)]
    for copy in ins:
        copy.start()
    for i in range(count):
        ins[i].wait()
        outs[i].start()
    for copy in outs:
        copy.wait()


def shards(features, weight_matrix, cotangent, block_rows, block_cols, blocks):
    assert lax.axis_size("row") == 16 and lax.axis_size("col") == 8
    count = blocks.shape[2]
    rows_dev, width = features.shape
    assert (rows_dev, width) == (512, 256) and blocks.shape[3] == 128 and count <= 128
    total_nodes = rows_dev * 128
    any_ = pl.BlockSpec(memory_space=pl.ANY)
    vmem = pl.BlockSpec(memory_space=pltpu.VMEM)
    out = [
        jax.ShapeDtypeStruct((4, 128, 256), F32),
        jax.ShapeDtypeStruct((256, 256), F32),
        jax.ShapeDtypeStruct((4, 128, 256), F32),
    ]
    scratch = [
        pltpu.VMEM((2, 64, 128, 128), F32),
        pltpu.VMEM((64, 128, 256), BF16),
        pltpu.VMEM((count, 128, 256), BF16),
        pltpu.VMEM((count, 128, 256), BF16),
        pltpu.VMEM((count, 128, 128), F32),
        pltpu.VMEM((2, 32, 128, 128), F32),
        pltpu.VMEM((2, 32, 128, 128), F32),
        pltpu.VMEM((2, 32, 128, 128), F32),
        pltpu.VMEM((2, 2, 2, 2, 128, 128), F32),
        pltpu.VMEM((2, 2, 2, 4, 128, 128), F32),
        pltpu.VMEM((2, 4, 128, 128), F32),
        pltpu.VMEM((2, 2, 2, 2, 128, 128), F32),
        pltpu.VMEM((2, 2, 2, 4, 128, 128), F32),
        pltpu.VMEM((2, 4, 128, 128), F32),
        pltpu.VMEM((256, 256), F32),
        pltpu.VMEM((4, 128, 256), F32),
        pltpu.VMEM((4, 128, 256), F32),
        pltpu.VMEM((4, 128, 256), F32),
        pltpu.VMEM((4, 128, 256), F32),
        pltpu.VMEM((256, 256), F32),
        pltpu.VMEM((128, 256), F32),
        pltpu.VMEM((8, 16, 256), F32),
        pltpu.VMEM((8, 16, 256), F32),
        pltpu.VMEM((256, 256), F32),
        pltpu.VMEM((4, 256, 256), BF16),
        pltpu.VMEM((2, 8, 128), jnp.int32),
        pltpu.VMEM((16, 128), jnp.int32),
        pltpu.SMEM((16, 128), jnp.int32),
        pltpu.SemaphoreType.DMA((N_SEM,)),
        pltpu.SemaphoreType.DMA((N_SEM,)),
        pltpu.SemaphoreType.DMA((16,)),
    ]
    made = pl.pallas_call(
        lambda *refs: kernel(total_nodes, *refs),
        out_shape=out,
        in_specs=[any_, any_, any_, vmem, vmem, any_],
        out_specs=[any_] * 3,
        scratch_shapes=scratch,
        compiler_params=pltpu.CompilerParams(
            collective_id=0, has_side_effects=True, vmem_limit_bytes=63 * 1024 * 1024
        ),
        name="graph_layer",
    )(
        features.reshape(4, 128, width),
        weight_matrix,
        cotangent.reshape(4, 128, width),
        block_rows[0],
        block_cols[0],
        blocks[0, 0],
    )
    hidden, weight_grad, feature_grad = pl.pallas_call(
        hand_over,
        out_shape=out,
        in_specs=[any_] * 3,
        out_specs=[any_] * 3,
        scratch_shapes=[pltpu.VMEM(a.shape, F32) for a in out] + [pltpu.SemaphoreType.DMA((3,))] * 2,
        name="hand_over",
    )(*made)
    return hidden.reshape(rows_dev, width), weight_grad, feature_grad.reshape(rows_dev, width)


def solution(mesh):
    in_specs = (
        P(("col", "row"), None),
        P(),
        P(("row", "col"), None),
        P("row", "col", None),
        P("row", "col", None),
        P("row", "col", None, None, None),
    )
    out_specs = (P(("row", "col"), None), P(), P(("col", "row"), None))
    return jax.shard_map(shards, mesh=mesh, in_specs=in_specs, out_specs=out_specs, check_vma=False)
```

```python
import math
import jax
import jax.numpy as jnp
from jax import lax
from jax.experimental import pallas as pl
from jax.experimental.pallas import tpu as pltpu
from jax.sharding import PartitionSpec as P

F32 = jnp.float32
BF16 = jnp.bfloat16
MESH = pl.DeviceIdType.MESH
HA = 0
HB = 2
N_SEM = 192
FAR = 1 << 20


def split(value):
    high = value.astype(BF16)
    return high, (value - high.astype(F32)).astype(BF16)


def dot(a, b):
    return jnp.dot(a, b, preferred_element_type=F32)


def dot3(ah, al, bh, bl):
    return dot(ah, bh) + dot(al, bh) + dot(ah, bl)


def sort_tables(ids, table, base, scratch, other, sources):
    count = ids.shape[-1]
    scratch[...] = jnp.full(scratch.shape, FAR, jnp.int32)
    scratch[0:1, 0:count] = ids
    scratch[1:2, 0:count] = other
    lane_ids = jnp.broadcast_to(scratch[0:1, :], (128, 128))
    lane_other = jnp.broadcast_to(scratch[1:2, :], (128, 128))
    sub_ids, sub_other = lane_ids.T, lane_other.T
    lane = lax.broadcasted_iota(jnp.int32, (128, 128), 1)
    sub = lax.broadcasted_iota(jnp.int32, (128, 128), 0)

    def total(mask, value, axis):
        return jnp.sum(jnp.where(mask, value, 0), axis=axis, keepdims=True)

    rank = total((lane_ids < sub_ids) | ((lane_ids == sub_ids) & (lane < sub)), 1, 1)
    below = total(lane_ids < sub_ids, 1, 1)
    here = (jnp.broadcast_to(rank, (128, 128)) == lane) & (sub < count)
    order = total(here, sub, 0)
    source = total(here, sub_other, 0)
    starts = total(here, jnp.broadcast_to(below, (128, 128)), 0)
    upto = total(sub_ids <= lane, 1, 0)
    same = total(sub_ids == lane, 1, 0)
    table[base : base + 1, :] = jnp.clip(order, 0, count - 1)
    table[base + 1 : base + 2, :] = jnp.clip(source, 0, sources - 1)
    table[base + 2 : base + 3, :] = jnp.where(starts == lane[0:1, :], 1, 0)
    table[base + 3 : base + 4, :] = jnp.clip(upto - 1, 0, count - 1)
    table[base + 4 : base + 5, :] = jnp.where(same > 0, 1, 0)


class Links:
    def __init__(self, send_sem, recv_sem):
        self.send_sem, self.recv_sem, self.used, self.open = send_sem, recv_sem, 0, []

    def send(self, src, dst, device):
        i = self.used
        self.used += 1
        assert i < N_SEM
        copy = pltpu.make_async_remote_copy(
            src_ref=src, dst_ref=dst, send_sem=self.send_sem.at[i], recv_sem=self.recv_sem.at[i],
            device_id=device, device_id_type=MESH)
        copy.start()
        self.open.append(copy)
        return copy

    def flush(self):
        for copy in self.open:
            copy.wait_send()
        self.open = []


class GatherRing:
    def __init__(self, links, view, pos, plus, minus, size, cross=None):
        self.links, self.view, self.pos, self.plus, self.minus = links, view, pos, plus, minus
        self.half, self.cross = size // 2, cross
        self.left, self.right, self.across = lax.rem(pos + 3, 4), lax.rem(pos + 1, 4), lax.rem(pos + 2, 4)

    def pieces(self, pos):
        return self.view(pos, 0, self.half), self.view(pos, self.half, self.half)

    def start(self):
        send = self.links.send
        a, b = self.pieces(self.pos)
        self.c1 = send(a, a, self.plus)
        self.c2 = send(b, b, self.minus)
        self.c3 = send(b, b, self.plus)
        self.c4 = send(a, a, self.minus)

    def relay(self):
        send = self.links.send
        self.c1.wait_recv()
        a = self.pieces(self.left)[0]
        self.r1 = send(a, a, self.plus)
        self.c2.wait_recv()
        b = self.pieces(self.right)[1]
        self.r2 = send(b, b, self.minus)
        if self.cross:
            self.crossed = [send(b, b, self.cross)]

    def cross_left(self):
        self.c3.wait_recv()
        b = self.pieces(self.left)[1]
        self.crossed.append(self.links.send(b, b, self.cross))

    def cross_far(self):
        self.r2.wait_recv()
        b = self.pieces(self.across)[1]
        self.crossed.append(self.links.send(b, b, self.cross))

    def finish(self, arrived=None, crossed=()):
        if not self.cross:
            self.c3.wait_recv()
            self.r2.wait_recv()
        self.c4.wait_recv()
        self.r1.wait_recv()
        for copy in crossed:
            copy.wait_recv()
        if arrived:
            for pos in (self.left, self.right, self.across):
                arrived(self.view(pos, HA, 4))


class SumRing:
    def __init__(self, links, view, near, far, pos, plus, minus):
        self.links, self.view, self.near, self.far = links, view, near, far
        self.pos, self.plus, self.minus = pos, plus, minus

    def start(self):
        view, q, send = self.view, self.pos, self.links.send
        left, right, across = lax.rem(q + 3, 4), lax.rem(q + 1, 4), lax.rem(q + 2, 4)
        self.o1 = send(view(across, HA, 2), self.near.at[0], self.plus)
        self.o2 = send(view(across, HB, 2), self.near.at[1], self.minus)
        self.n1 = send(view(right, HB, 2), self.far.at[0, 2:4], self.plus)
        self.n2 = send(view(left, HA, 2), self.far.at[1, 0:2], self.minus)

    def relay(self):
        view, q, send = self.view, self.pos, self.links.send
        left, right = lax.rem(q + 3, 4), lax.rem(q + 1, 4)
        self.o1.wait_recv()
        part = view(right, HA, 2)
        part[...] += self.near[0]
        self.m1 = send(part, self.far.at[0, 0:2], self.plus)
        self.o2.wait_recv()
        part = view(left, HB, 2)
        part[...] += self.near[1]
        self.m2 = send(part, self.far.at[1, 2:4], self.minus)

    def finish(self):
        self.n1.wait_recv()
        self.n2.wait_recv()
        self.m1.wait_recv()
        self.m2.wait_recv()
        part = self.view(self.pos, HA, 4)
        part[...] += self.far[0] + self.far[1]
        return part


def kernel(total_nodes, feats, weight, cot, rows_in, cols_in, blocks, hidden_out, wgrad_out, fgrad_out,
           X, XX, A, AT, PS, OUT, BK, DR, CN, CF, CX, RN, RF, RX, W_ref, C_ref, AG, DP, HID, G, WH, WR, WS, WO,
           WP, IDS, TAB, TABS, send_sem, recv_sem, load_sem):
    row, col = lax.axis_index("row"), lax.axis_index("col")
    y, x_lo, core = row // 4, lax.rem(row // 2, 2), lax.rem(row, 2)
    z, x_hi = col // 2, lax.rem(col, 2)
    chip = row // 2

    def at_row(yy, xx, cc):
        return (yy * 4 + xx * 2 + cc, col)

    def at_col(zz, xx):
        return (row, zz * 2 + xx)

    y_plus, y_minus = at_row(lax.rem(y + 1, 4), x_lo, core), at_row(lax.rem(y + 3, 4), x_lo, core)
    z_plus, z_minus = at_col(lax.rem(z + 1, 4), x_hi), at_col(lax.rem(z + 3, 4), x_hi)
    x_near, twin, x_far = at_row(y, 1 - x_lo, core), at_row(y, x_lo, 1 - core), at_col(z, 1 - x_hi)
    col_peers = [(row, lax.rem(col + j, 8)) for j in range(1, 8)]
    row_peers = [(lax.rem(chip + j, 8) * 2 + core, col) for j in range(1, 8)]

    loads = []

    def load(src, dst):
        copy = pltpu.make_async_copy(src, dst, load_sem.at[len(loads)])
        copy.start()
        loads.append(copy)
        return copy

    lanes = [pl.ds(f * 128, 128) for f in range(2)]
    mine_x = [X.at[f, pl.ds(row * 4, 4)] for f in range(2)]
    get_x = [load(feats.at[:, :, lanes[f]], mine_x[f]) for f in range(2)]
    get_a = load(blocks, PS)
    get_w = load(weight, W_ref)
    get_c = load(cot, C_ref)

    barrier = pltpu.get_barrier_semaphore()
    peers = col_peers + row_peers + [twin]
    for peer in peers:
        pl.semaphore_signal(barrier, inc=1, device_id=peer, device_id_type=MESH)
    pl.semaphore_wait(barrier, len(peers))

    links = Links(send_sem, recv_sem)
    send = links.send

    def x_view(f, xx):
        return lambda q, half, n: X.at[f, pl.ds((q * 4 + xx * 2 + core) * 4 + half, n)]

    own = [GatherRing(links, x_view(f, x_lo), y, y_plus, y_minus, 4, x_near) for f in range(2)]
    other = [GatherRing(links, x_view(f, 1 - x_lo), y, y_plus, y_minus, 2) for f in range(2)]
    xs, twins = [None, None], [[], []]

    def to_twin(f):
        return lambda piece: twins[f].append(send(piece, piece, twin))

    def across(view, pos, device):
        return [send(view(pos, half, 2), view(pos, half, 2), device) for half in (HA, HB)]

    get_x[0].wait()
    xs[0] = across(x_view(0, x_lo), y, x_near)
    own[0].start()
    get_x[1].wait()
    to_twin(0)(mine_x[0])
    to_twin(1)(mine_x[1])

    sort_tables(rows_in[...], TAB, 0, IDS.at[0], cols_in[...], 64)
    sort_tables(cols_in[...], TAB, 8, IDS.at[1], rows_in[...], 32)
    get_tab = load(TAB, TABS)
    get_tab.wait()
    get_a.wait()

    def prepare(k, carry):
        value = PS[k]
        high, low = split(value)
        A[k, :, 0:128] = high
        A[k, :, 128:256] = low
        high, low = split(value.T)
        AT[k, :, 0:128] = high
        AT[k, :, 128:256] = low
        return carry

    own[0].relay()
    xs[0][0].wait_recv()
    other[0].start()
    lax.fori_loop(0, 16, prepare, 0, unroll=2)
    own[0].cross_left()
    xs[0][1].wait_recv()
    to_twin(0)(x_view(0, 1 - x_lo)(y, HA, 4))
    lax.fori_loop(16, 48, prepare, 0, unroll=2)
    other[0].relay()
    own[0].cross_far()
    own[1].start()
    xs[1] = across(x_view(1, x_lo), y, x_near)
    lax.fori_loop(48, 96, prepare, 0, unroll=2)
    get_w.wait()
    high, low = split(W_ref[...])
    WP[0], WP[1] = high, low
    high, low = split(W_ref[...].T)
    WP[2], WP[3] = high, low
    get_c.wait()

    def to_pairs(source, f, count):
        def step(k, carry):
            high, low = split(source[f, k])
            XX[k, :, 0:128] = high
            XX[k, :, 128:256] = low
            return carry

        lax.fori_loop(0, count, step, 0, unroll=4)

    def tile_product(left, base, between=None):
        def step(p, total):
            lhs = left[TABS[base, p]]
            pair = XX[TABS[base + 1, p]]
            result = dot(lhs, jnp.concatenate([pair, pair], axis=0))
            term = result[:, 0:128] + result[:, 128:256]
            total = jnp.where(TABS[base + 2, p] == 1, term, total + term)
            PS[p] = total
            return total

        middle = PS.shape[0] // 2
        total = lax.fori_loop(0, middle, step, jnp.zeros((128, 128), F32), unroll=16)
        if between:
            between()
        lax.fori_loop(middle, PS.shape[0], step, total, unroll=16)

    def collect(dst, f, base, start, count, place):
        def step(r, carry):
            t = place(r)
            dst[f, t] = jnp.where(TABS[base + 4, t] == 1, PS[TABS[base + 3, t]], 0.0)
            return carry

        lax.fori_loop(start, start + count, step, 0, unroll=4)

    def same(r):
        return r

    def col_view(f, xx):
        return lambda q, half, n: OUT.at[f, pl.ds((q * 2 + xx) * 4 + half, n)]

    col_far = [SumRing(links, col_view(f, 1 - x_hi), CN.at[f, 0], CF.at[f, 0], z, z_plus, z_minus) for f in range(2)]
    col_own = [SumRing(links, col_view(f, x_hi), CN.at[f, 1], CF.at[f, 1], z, z_plus, z_minus) for f in range(2)]

    def finish_gather(f):
        own[f].finish(to_twin(f))
        other[f].finish(to_twin(f), own[f].crossed)
        for copy in twins[f]:
            copy.wait_recv()

    def forward(f, between=None):
        to_pairs(X, f, X.shape[1])
        tile_product(A, 0, between)
        collect(OUT, f, 0, 0, OUT.shape[1], same)
        col_far[f].start()

    def next_half():
        own[1].relay()
        xs[1][0].wait_recv()
        other[1].start()

    finish_gather(0)
    forward(0, next_half)
    col_own[0].start()
    own[1].cross_left()
    xs[1][1].wait_recv()
    to_twin(1)(x_view(1, 1 - x_lo)(y, HA, 4))
    other[1].relay()
    own[1].cross_far()
    col_far[0].relay()
    finish_gather(1)
    col_own[0].relay()
    forward(1)
    sums = [send(col_far[0].finish(), CX.at[0], x_far)]
    col_own[0].finish()
    col_far[1].relay()
    col_own[1].start()
    sums.append(send(col_far[1].finish(), CX.at[1], x_far))
    col_own[1].relay()
    col_own[1].finish()
    for f in range(2):
        sums[f].wait_recv()

    early, links.open = links.open, []

    def middle(i, carry):
        agg0 = OUT[0, col * 4 + i] + CX[0, i]
        agg1 = OUT[1, col * 4 + i] + CX[1, i]
        agg = jnp.concatenate([agg0, agg1], axis=1)
        ah, al = split(agg)
        pre = dot3(ah, al, WP[0], WP[1])
        sig = 1.0 / (1.0 + jnp.exp(-pre))
        HID[i] = pre * sig
        dpre = C_ref[i] * sig * (1.0 + pre * (1.0 - sig))
        dh, dl = split(dpre)
        back = dot3(dh, dl, WP[2], WP[3])
        BK[0, col * 4 + i] = back[:, 0:128]
        BK[1, col * 4 + i] = back[:, 128:256]
        AG[i] = agg
        DP[i] = dpre
        return carry

    lax.fori_loop(0, 4, middle, 0)

    def b_view(f, xx):
        return lambda q, half, n: BK.at[f, pl.ds((q * 2 + xx) * 4 + half, n)]

    own = [GatherRing(links, b_view(f, x_hi), z, z_plus, z_minus, 4, x_far) for f in range(2)]
    other = [GatherRing(links, b_view(f, 1 - x_hi), z, z_plus, z_minus, 2) for f in range(2)]
    xs = [across(b_view(0, x_hi), z, x_far)]
    own[0].start()
    put_h = load(HID, hidden_out)

    def term(i, total):
        th, tl = split(AG[i].T)
        dh, dl = split(DP[i])
        return total + dot3(th, tl, dh, dl)

    G[...] = lax.fori_loop(0, 4, term, jnp.zeros(G.shape, F32)) / jnp.float32(math.sqrt(total_nodes))
    half_of = lambda c: pl.ds(pl.multiple_of(c * 128, 128), 128)
    w1 = send(G.at[half_of(1 - core)], WH, twin)

    own[0].relay()
    xs[0][0].wait_recv()
    other[0].start()
    w1.wait_recv()
    WH[...] += G[half_of(core), :]
    slot = lambda m: pl.ds(pl.multiple_of(m * 16, 16), 16)
    w2 = [send(WH.at[slot(peer[1])], WR.at[col], peer) for peer in col_peers]
    WR[col] = WH[slot(col), :]
    own[0].cross_left()
    other[0].relay()
    own[0].cross_far()
    own[1].start()
    xs.append(across(b_view(1, x_hi), z, x_far))
    for copy in w2:
        copy.wait_recv()

    def add_all(parts):
        total = parts[0]
        for m in range(1, 8):
            total = total + parts[m]
        return total

    WS[chip] = add_all(WR)
    w3 = [send(WS.at[chip], WS.at[chip], peer) for peer in row_peers]

    def r_view(f, xx, cc):
        return lambda q, half, n: X.at[f, pl.ds((q * 4 + xx * 2 + cc) * 4 + half, n)]

    def part(xx, cc):
        return lambda r: ((r // 4) * 4 + xx * 2 + cc) * 4 + lax.rem(r, 4)

    row_far = [SumRing(links, r_view(f, 1 - x_lo, core), RN.at[f, 0], RF.at[f, 0], y, y_plus, y_minus) for f in range(2)]
    row_own = [SumRing(links, r_view(f, x_lo, core), RN.at[f, 1], RF.at[f, 1], y, y_plus, y_minus) for f in range(2)]

    def finish_back(f):
        own[f].finish()
        xs[f][1].wait_recv()
        other[f].finish(None, own[f].crossed)

    for copy in early:
        copy.wait_send()

    def backward(f, between=None):
        to_pairs(BK, f, BK.shape[1])
        tile_product(AT, 8, between)

        moves = []
        for k, xx in enumerate((1 - x_lo, x_lo)):
            collect(X, f, 8, 0, 16, part(xx, 1 - core))
            for m in range(4):
                moves.append(send(r_view(f, xx, 1 - core)(m, HA, 4), DR.at[f, pl.ds(k * 16 + m * 4, 4)], twin))
        for xx in (1 - x_lo, x_lo):
            collect(X, f, 8, 0, 16, part(xx, core))
        return moves

    def join(f, moves, k):
        for copy in moves[k * 4 : k * 4 + 4]:
            copy.wait_recv()
        place = part(x_lo if k else 1 - x_lo, core)

        def step(r, carry):
            X[f, place(r)] += DR[f, k * 16 + r]
            return carry

        lax.fori_loop(0, 16, step, 0, unroll=4)

    finish_back(0)
    moves = backward(0, next_half)
    own[1].cross_left()
    join(0, moves, 0)
    row_far[0].start()
    other[1].relay()
    own[1].cross_far()
    join(0, moves, 1)
    row_own[0].start()
    for copy in w3:
        copy.wait_recv()
    mine_w = WO.at[pl.ds(pl.multiple_of(core * 128 + col * 16, 16), 16)]
    mine_w[...] = add_all(WS)
    w4 = [send(mine_w, mine_w, peer) for peer in col_peers]
    row_far[0].relay()
    finish_back(1)
    moves = backward(1)
    row_own[0].relay()
    sums = [send(row_far[0].finish(), RX.at[0], x_near)]
    join(1, moves, 0)
    row_far[1].start()
    join(1, moves, 1)
    for copy in w4:
        copy.wait_recv()
    w5 = send(WO.at[half_of(core)], WO.at[half_of(core)], twin)
    row_own[0].finish()
    row_far[1].relay()
    row_own[1].start()
    w5.wait_recv()
    put_w = load(WO, wgrad_out)
    sums[0].wait_recv()
    mine_x[0][...] += RX[0]
    put_0 = load(mine_x[0], fgrad_out.at[:, :, lanes[0]])
    sums.append(send(row_far[1].finish(), RX.at[1], x_near))
    row_own[1].relay()
    row_own[1].finish()
    sums[1].wait_recv()
    mine_x[1][...] += RX[1]
    put_1 = load(mine_x[1], fgrad_out.at[:, :, lanes[1]])
    links.flush()
    for copy in (put_h, put_w, put_0, put_1):
        copy.wait()


def hand_over(*refs):
    count = len(refs) // 3
    sources, results, held = refs[:count], refs[count : 2 * count], refs[2 * count : 3 * count]
    in_sem, out_sem = refs[3 * count :]
    ins = [pltpu.make_async_copy(sources[i], held[i], in_sem.at[i]) for i in range(count)]
    outs = [pltpu.make_async_copy(held[i], results[i], out_sem.at[i]) for i in range(count)]
    for copy in ins:
        copy.start()
    for i in range(count):
        ins[i].wait()
        outs[i].start()
    for copy in outs:
        copy.wait()


def shards(features, weight_matrix, cotangent, block_rows, block_cols, blocks):
    assert lax.axis_size("row") == 16 and lax.axis_size("col") == 8
    count = blocks.shape[2]
    rows_dev, width = features.shape
    assert (rows_dev, width) == (512, 256) and blocks.shape[3] == 128 and count <= 128
    total_nodes = rows_dev * 128
    any_ = pl.BlockSpec(memory_space=pl.ANY)
    vmem = pl.BlockSpec(memory_space=pltpu.VMEM)
    out = [
        jax.ShapeDtypeStruct((4, 128, 256), F32),
        jax.ShapeDtypeStruct((256, 256), F32),
        jax.ShapeDtypeStruct((4, 128, 256), F32),
    ]
    scratch = [
        pltpu.VMEM((2, 64, 128, 128), F32),
        pltpu.VMEM((64, 128, 256), BF16),
        pltpu.VMEM((count, 128, 256), BF16),
        pltpu.VMEM((count, 128, 256), BF16),
        pltpu.VMEM((count, 128, 128), F32),
        pltpu.VMEM((2, 32, 128, 128), F32),
        pltpu.VMEM((2, 32, 128, 128), F32),
        pltpu.VMEM((2, 32, 128, 128), F32),
        pltpu.VMEM((2, 2, 2, 2, 128, 128), F32),
        pltpu.VMEM((2, 2, 2, 4, 128, 128), F32),
        pltpu.VMEM((2, 4, 128, 128), F32),
        pltpu.VMEM((2, 2, 2, 2, 128, 128), F32),
        pltpu.VMEM((2, 2, 2, 4, 128, 128), F32),
        pltpu.VMEM((2, 4, 128, 128), F32),
        pltpu.VMEM((256, 256), F32),
        pltpu.VMEM((4, 128, 256), F32),
        pltpu.VMEM((4, 128, 256), F32),
        pltpu.VMEM((4, 128, 256), F32),
        pltpu.VMEM((4, 128, 256), F32),
        pltpu.VMEM((256, 256), F32),
        pltpu.VMEM((128, 256), F32),
        pltpu.VMEM((8, 16, 256), F32),
        pltpu.VMEM((8, 16, 256), F32),
        pltpu.VMEM((256, 256), F32),
        pltpu.VMEM((4, 256, 256), BF16),
        pltpu.VMEM((2, 8, 128), jnp.int32),
        pltpu.VMEM((16, 128), jnp.int32),
        pltpu.SMEM((16, 128), jnp.int32),
        pltpu.SemaphoreType.DMA((N_SEM,)),
        pltpu.SemaphoreType.DMA((N_SEM,)),
        pltpu.SemaphoreType.DMA((16,)),
    ]
    made = pl.pallas_call(
        lambda *refs: kernel(total_nodes, *refs),
        out_shape=out,
        in_specs=[any_, any_, any_, vmem, vmem, any_],
        out_specs=[any_] * 3,
        scratch_shapes=scratch,
        compiler_params=pltpu.CompilerParams(
            collective_id=0, has_side_effects=True, vmem_limit_bytes=63 * 1024 * 1024
        ),
        name="graph_layer",
    )(
        features.reshape(4, 128, width),
        weight_matrix,
        cotangent.reshape(4, 128, width),
        block_rows[0],
        block_cols[0],
        blocks[0, 0],
    )
    hidden, weight_grad, feature_grad = pl.pallas_call(
        hand_over,
        out_shape=out,
        in_specs=[any_] * 3,
        out_specs=[any_] * 3,
        scratch_shapes=[pltpu.VMEM(a.shape, F32) for a in out] + [pltpu.SemaphoreType.DMA((3,))] * 2,
        name="hand_over",
    )(*made)
    return hidden.reshape(rows_dev, width), weight_grad, feature_grad.reshape(rows_dev, width)


def solution(mesh):
    in_specs = (
        P(("col", "row"), None),
        P(),
        P(("row", "col"), None),
        P("row", "col", None),
        P("row", "col", None),
        P("row", "col", None, None, None),
    )
    out_specs = (P(("row", "col"), None), P(), P(("col", "row"), None))
    return jax.shard_map(shards, mesh=mesh, in_specs=in_specs, out_specs=out_specs, check_vma=False)
```
